32 devices in a mesh: dp: 2 (over x), ctx: 4 (over y, core), tensor: 4 (over z).
Axes of the slice: x: 2, y: 2, z: 4, core: 2. Of those that a mesh axis runs over, the one named last changes fastest.
Arguments:
- hidden: bfloat16 [2, 16384, 2560], P('dp', 'ctx', 'tensor'), may hold values from -6 to 6
- depth: int32 [2, 16384], P('dp', 'ctx'), may hold values from 1 to 4, as said below
- qkv_weight: bfloat16 [2560, 3, 2560], P(None, None, 'tensor'), may hold values from -0.125 to 0.125
- out_weight: bfloat16 [2560, 2560], P('tensor'), may hold values from -0.125 to 0.125
Outputs:
- update: bfloat16 [2, 16384, 2560], P('dp', 'ctx', 'tensor')
The draws below stay inside these ranges and needn't reach their ends.
Inputs may be any that keep to these rules, and one draw needn't show every extreme that they name: In every aligned block of 4096 positions of a document at most 1024 tokens have depth at least 3, and some block has exactly 1024; over all documents exactly 4096 tokens do.
All inputs are finite; a program needn't handle non-finite values.
Results may differ from the reference program's by a relative error of at most 0.012.
The reference program's roundings to bfloat16 on the way count: a program that leaves them out, or rounds other values in their place, can miss the bound.
Values may be sent and summed in bfloat16 or wider, within the bound.
A program may use at most 256 MiB of HBM per device.

```python
import jax
import jax.numpy as jnp
from jax import lax

D = 2560
HEADS = 20
HD = 128
RECURSION = 3
MAX_DEPTH = 4
TOK_DEV = 4096
ACT_DEV = 512
CAP = 1024
DOCS = 2
LEN = 16384
N_DP = 2
N_CTX = 4
N_TENSOR = 4


def draw_depth(key, part):
    shard_total = DOCS * (LEN // TOK_DEV)
    half_total = shard_total // 2
    key_order, key_load, key_place, key_deep, key_shallow = jax.random.split(jax.random.fold_in(key, 17), 5)
    loads = jax.random.randint(key_load, (half_total,), 0, CAP + 1)
    loads = loads.at[0].set(CAP)
    paired = jnp.concatenate([loads, CAP - loads])
    shuffled = jax.random.permutation(key_order, shard_total)
    shard_counts = jnp.zeros((shard_total,), jnp.int32).at[shuffled].set(paired.astype(jnp.int32))
    place_keys = jax.random.split(key_place, shard_total)
    ranking = jax.vmap(lambda single: jax.random.permutation(single, TOK_DEV))(place_keys)
    chosen = ranking < shard_counts[:, None]
    deeper = jax.random.randint(key_deep, (shard_total, TOK_DEV), RECURSION, MAX_DEPTH + 1)
    shallow = jax.random.randint(key_shallow, (shard_total, TOK_DEV), 1, RECURSION)
    return jnp.where(chosen, deeper, shallow).reshape(DOCS, LEN).astype(jnp.int32)


def levels(rng, shape, cuts, low, largest):
    def one(axis_at, parts):
        draws = jax.random.uniform(jax.random.fold_in(jax.random.fold_in(rng, 6), axis_at), (parts,), jnp.float32, low / len(cuts), largest / len(cuts))
        return jnp.repeat(jnp.exp(draws), shape[axis_at] // parts).reshape((-1,) + (1,) * (len(shape) - axis_at - 1))

    factor_of = one(*cuts[0])
    for cut in cuts[1:]:
        factor_of = factor_of * one(*cut)
    return factor_of


def bell_draw(stream_key, shape, scale, limit, pieces=(), kind=jnp.bfloat16):
    array = scale * jax.random.normal(stream_key, shape, jnp.float32)
    if pieces:
        array = array * levels(stream_key, shape, pieces, -0.22, 0.18)
    return jnp.clip(array, -limit, limit).astype(kind)


def setup_inputs(seed: int = 0) -> dict:
    streams_of = jax.random.split(jax.random.key(seed), 5)
    return {
        "hidden": bell_draw(streams_of[0], (DOCS, LEN, D), 1.0, 6.0, ((0, 2), (1, 4), (2, 4))),
        "depth": draw_depth(jax.random.fold_in(streams_of[4], 71), 0),
        "qkv_weight": bell_draw(streams_of[2], (D, 3, HEADS * HD), D ** -0.5, 0.125, ((2, 4),)),
        "out_weight": bell_draw(streams_of[3], (HEADS * HD, D), (HEADS * HD) ** -0.5, 0.125, ((0, 4),)),
    }


score_scale = 0.25
norm_epsilon = 1e-05
head_epsilon = 1e-06

def head_normed(values):
    row_count = values.shape[0]
    per_head = values.reshape(row_count, -1, HD)
    factor = lax.rsqrt(lax.optimization_barrier(jnp.mean(per_head * per_head, axis=2, keepdims=True)) + head_epsilon)
    return (per_head * factor).reshape(row_count, -1).astype(jnp.bfloat16)

def reference(hidden, depth, qkv_weight, out_weight):
    doc_total, length, feature_width = hidden.shape
    head_width = qkv_weight.shape[2]
    active_total = ACT_DEV * N_DP * N_CTX
    doc_room = min(length, N_CTX * CAP)
    active = depth >= RECURSION
    doc_counts = lax.optimization_barrier(jnp.sum(active.astype(jnp.int32), axis=1)).astype(jnp.int32)
    doc_starts = (jnp.cumsum(doc_counts) - doc_counts).astype(jnp.int32)
    flat_index = jnp.nonzero(active.reshape(-1), size=active_total, fill_value=0)[0].astype(jnp.int32)
    token_rows = hidden.reshape(-1, feature_width)[flat_index].astype(jnp.float32)
    factor = lax.rsqrt(lax.optimization_barrier(jnp.mean(token_rows * token_rows, axis=1, keepdims=True)) + norm_epsilon)
    normed = (token_rows * factor).astype(jnp.bfloat16)
    projection = jnp.dot(normed, qkv_weight.reshape(feature_width, 3 * head_width), preferred_element_type=jnp.float32)
    queries = head_normed(projection[:, :head_width])
    key_rows = head_normed(projection[:, head_width:2 * head_width])
    value_rows = projection[:, 2 * head_width:].astype(jnp.bfloat16)
    positions = (flat_index % length).astype(jnp.int32)
    doc_of = (flat_index // length).astype(jnp.int32)
    padding = jnp.zeros((doc_room, head_width), jnp.bfloat16)
    padded_queries = jnp.concatenate([queries, padding], axis=0)
    padded_keys = jnp.concatenate([key_rows, padding], axis=0)
    padded_values = jnp.concatenate([value_rows, padding], axis=0)
    padded_positions = jnp.concatenate([positions, jnp.zeros((doc_room,), jnp.int32)], axis=0)

    def one_document(doc_number):
        doc_begin = doc_starts[doc_number]
        query_block = lax.dynamic_slice_in_dim(padded_queries, doc_begin, doc_room).astype(jnp.float32).reshape(doc_room, -1, HD)
        key_block = lax.dynamic_slice_in_dim(padded_keys, doc_begin, doc_room).astype(jnp.float32).reshape(doc_room, -1, HD)
        value_block = lax.dynamic_slice_in_dim(padded_values, doc_begin, doc_room).astype(jnp.float32).reshape(doc_room, -1, HD)
        position_block = lax.dynamic_slice_in_dim(padded_positions, doc_begin, doc_room)
        filled = jnp.arange(doc_room, dtype=jnp.int32) < doc_counts[doc_number]
        allowed = filled[:, None] & filled[None, :] & (position_block[None, :] <= position_block[:, None])
        scores = jnp.einsum('qhd,khd->hqk', query_block, key_block) * score_scale
        weights = jnp.where(allowed[None], jnp.exp(scores), 0.0)
        rounded = lax.optimization_barrier(weights.astype(jnp.bfloat16)).astype(jnp.float32)
        numerator = jnp.einsum('hqk,khd->qhd', rounded, value_block)
        denominator = lax.optimization_barrier(jnp.sum(weights, axis=2)) + (1.0 - filled.astype(jnp.float32))[None, :]
        context = numerator / jnp.transpose(denominator)[:, :, None]
        return context.reshape(doc_room, head_width).astype(jnp.bfloat16)
    contexts = lax.map(one_document, jnp.arange(doc_total, dtype=jnp.int32))
    within = (jnp.arange(active_total, dtype=jnp.int32) - doc_starts[doc_of]).astype(jnp.int32)
    context_rows = contexts[doc_of, within]
    group_width = head_width // N_TENSOR
    summed = jnp.zeros((active_total, feature_width), jnp.float32)
    for group_index in range(N_TENSOR):
        lower = group_index * group_width
        partial_value = jnp.dot(context_rows[:, lower:lower + group_width], out_weight[lower:lower + group_width], preferred_element_type=jnp.float32).astype(jnp.bfloat16)
        summed = summed + lax.optimization_barrier(partial_value).astype(jnp.float32)
    update = jnp.zeros((doc_total * length, feature_width), jnp.bfloat16).at[flat_index].set(summed.astype(jnp.bfloat16))
    return update.reshape(doc_total, length, feature_width)
```

```python
import functools

import jax
import jax.numpy as jnp
from jax import lax
from jax.experimental import pallas as pl
from jax.experimental.pallas import tpu as pltpu
from jax.sharding import PartitionSpec as P

HD = 128
RECURSION = 3
CAP = 1024
ACT_DEV = 512

score_scale = 0.25
norm_epsilon = 1e-05
head_epsilon = 1e-06
VMEM_LIMIT = 60 * 1024 * 1024
PLANE = ("dp", "ctx")


def project_kernel(x_ref, w_ref, q_ref, kv_ref, normed):
    part = pl.program_id(0)
    shards, rows, width = x_ref.shape

    @pl.when(part == 0)
    def _():
        total = jnp.zeros((rows, 1), jnp.float32)
        for z in range(shards):
            wide = x_ref[z].astype(jnp.float32)
            total = total + jnp.sum(wide * wide, axis=1, keepdims=True)
        factor = lax.rsqrt(total / (shards * width) + norm_epsilon)
        for z in range(shards):
            normed[z] = (x_ref[z].astype(jnp.float32) * factor).astype(jnp.bfloat16)

    acc = jnp.dot(normed[0], w_ref[0, :width], preferred_element_type=jnp.float32)
    for z in range(1, shards):
        acc = acc + jnp.dot(normed[z], w_ref[0, z * width : (z + 1) * width], preferred_element_type=jnp.float32)
    heads = acc.shape[1] // HD

    def head_normed(scale):
        parts = []
        for h in range(heads):
            head = acc[:, h * HD : (h + 1) * HD]
            factor = lax.rsqrt(jnp.mean(head * head, axis=1, keepdims=True) + head_epsilon) * scale
            parts.append((head * factor).astype(jnp.bfloat16))
        return parts

    @pl.when(part == 0)
    def _():
        for h, value in enumerate(head_normed(score_scale)):
            q_ref[:, h * HD : (h + 1) * HD] = value

    @pl.when(part == 1)
    def _():
        for h, value in enumerate(head_normed(1.0)):
            kv_ref[0, :, h * HD : (h + 1) * HD] = value

    @pl.when(part == 2)
    def _():
        kv_ref[0] = acc.astype(jnp.bfloat16)


def project(rows_all, weight):
    shards, rows, width = rows_all.shape
    head_width = weight.shape[2]
    flops = 2 * rows * shards * width * 3 * head_width
    return pl.pallas_call(
        project_kernel,
        grid=(3,),
        out_shape=[
            jax.ShapeDtypeStruct((rows, head_width), jnp.bfloat16),
            jax.ShapeDtypeStruct((2, rows, head_width), jnp.bfloat16),
        ],
        in_specs=[
            pl.BlockSpec((shards, rows, width), lambda p: (0, 0, 0)),
            pl.BlockSpec((1, shards * width, head_width), lambda p: (p, 0, 0)),
        ],
        out_specs=[
            pl.BlockSpec((rows, head_width), lambda p: (0, 0)),
            pl.BlockSpec((1, rows, head_width), lambda p: (jnp.maximum(p - 1, 0), 0, 0)),
        ],
        scratch_shapes=[pltpu.VMEM((shards, rows, width), jnp.bfloat16)],
        compiler_params=pltpu.CompilerParams(vmem_limit_bytes=VMEM_LIMIT),
        cost_estimate=pl.CostEstimate(flops=flops, bytes_accessed=2 * weight.size, transcendentals=0),
        name="project",
    )(rows_all, weight)


def gather_kernel(pieces, kv_ref, out_ref, send_sem, recv_sem, local_sem):
    x, place = lax.axis_index("dp"), lax.axis_index("ctx")
    y, core = place // 2, lax.rem(place, 2)
    rows = kv_ref.shape[1] // pieces

    def block(flip_x, flip_y, flip_core):
        return (x ^ flip_x) * 4 + (y ^ flip_y) * 2 + (core ^ flip_core)

    def device(flip_x, flip_y, flip_core):
        return {"dp": x ^ flip_x, "ctx": (y ^ flip_y) * 2 + (core ^ flip_core)}

    sibling, across_x, across_y = device(0, 0, 1), device(1, 0, 0), device(0, 1, 0)
    barrier = pltpu.get_barrier_semaphore()
    for target in (sibling, across_x, across_y):
        pl.semaphore_signal(barrier, inc=1, device_id=target, device_id_type=pl.DeviceIdType.MESH)
    pl.semaphore_wait(barrier, 3)

    me = block(0, 0, 0)
    local = pltpu.make_async_copy(kv_ref, out_ref.at[me], local_sem)
    local.start()
    sends = []

    def send(origin, route, piece, target, own=False):
        window = pl.ds(piece * rows, rows)
        copy = pltpu.make_async_remote_copy(
            src_ref=kv_ref.at[:, window] if own else out_ref.at[origin, :, window],
            dst_ref=out_ref.at[origin, :, window],
            send_sem=send_sem.at[route, piece],
            recv_sem=recv_sem.at[route, piece],
            device_id=target,
            device_id_type=pl.DeviceIdType.MESH,
        )
        copy.start()
        sends.append(copy)

    def arrive(origin, route, piece):
        window = pl.ds(piece * rows, rows)
        pltpu.make_async_remote_copy(
            src_ref=out_ref.at[origin, :, window],
            dst_ref=out_ref.at[origin, :, window],
            send_sem=send_sem.at[route, piece],
            recv_sem=recv_sem.at[route, piece],
            device_id=sibling,
            device_id_type=pl.DeviceIdType.MESH,
        ).wait_recv()

    for piece in range(pieces):
        send(me, 1, piece, across_x, True)
        send(me, 2, piece, across_y, True)
        send(me, 0, piece, sibling, True)
    first = core == 0
    onward = jnp.where(first, block(0, 1, 0), block(1, 0, 0))
    onward_device = {
        "dp": jnp.where(first, x ^ 1, x),
        "ctx": jnp.where(first, place, (y ^ 1) * 2 + core),
    }
    for piece in range(pieces):
        arrive(block(1, 0, 0), 1, piece)
        arrive(block(0, 1, 0), 2, piece)
        send(onward, 3, piece, onward_device)
        send(block(1, 0, 0), 4, piece, sibling)
        send(block(0, 1, 0), 5, piece, sibling)
    for piece in range(pieces):
        arrive(block(1, 1, 0), 3, piece)
        send(block(1, 1, 0), 6, piece, sibling)
    for piece in range(pieces):
        arrive(block(0, 0, 1), 0, piece)
        arrive(block(1, 0, 1), 4, piece)
        arrive(block(0, 1, 1), 5, piece)
        arrive(block(1, 1, 1), 6, piece)
    for copy in sends:
        copy.wait_send()
    local.wait()


def gather_plane(kv, call):
    docs, ctx_count = lax.axis_size("dp"), lax.axis_size("ctx")
    if (docs, ctx_count) != (2, 4):
        return lax.all_gather(kv, PLANE, axis=0)
    pieces = 8
    plane = docs * ctx_count
    return pl.pallas_call(
        functools.partial(gather_kernel, pieces),
        out_shape=jax.ShapeDtypeStruct((plane,) + kv.shape, kv.dtype),
        in_specs=[pl.BlockSpec(memory_space=pltpu.VMEM)],
        out_specs=pl.BlockSpec(memory_space=pl.ANY),
        scratch_shapes=[
            pltpu.SemaphoreType.DMA((7, pieces)),
            pltpu.SemaphoreType.DMA((7, pieces)),
            pltpu.SemaphoreType.DMA,
        ],
        compiler_params=pltpu.CompilerParams(collective_id=call, has_side_effects=True),
        cost_estimate=pl.CostEstimate(flops=0, bytes_accessed=60_000_000, transcendentals=0),
        name="gather_plane",
    )(kv)


def attend_kernel(docs, base, meta_ref, q_ref, *refs):
    w_ref, o_ref, total = refs[-3:]
    pairs = [(refs[i], refs[i + 1]) for i in range(0, len(refs) - 3, 2)]
    head = pl.program_id(0)
    plane, stripes, size, _ = refs[0].shape
    period = plane * size
    rows = stripes * size
    me = meta_ref[docs]
    row = lax.broadcasted_iota(jnp.int32, (rows, 1), 0)
    q_index = (base + row // size) * period + me * size + lax.rem(row, size)
    begin = jnp.zeros((rows, 1), jnp.int32)
    for d in range(docs):
        begin = jnp.where(q_index >= meta_ref[d], meta_ref[d], begin)
    lane = lax.broadcasted_iota(jnp.int32, (1, period), 1)
    query = q_ref[...]
    num = jnp.zeros((rows, HD), jnp.float32)
    den = jnp.zeros((rows, 1), jnp.float32)
    at = 0
    for k_ref, v_ref in pairs:
        for k in range(stripes):
            keys = k_ref[:, k].reshape(period, HD)
            values = v_ref[:, k].reshape(period, HD)
            scores = lax.dot_general(query, keys, (((1,), (1,)), ((), ())), preferred_element_type=jnp.float32)
            allowed = lane >= begin - at * period
            if at >= base:
                allowed = allowed & (lane <= q_index - at * period)
            weights = jnp.where(allowed, jnp.exp(scores), 0.0)
            den = den + jnp.sum(weights, axis=1, keepdims=True)
            num = num + jnp.dot(weights.astype(jnp.bfloat16), values, preferred_element_type=jnp.float32)
            at += 1
    context = (num / den).astype(jnp.bfloat16)
    term = jnp.dot(context, w_ref[...], preferred_element_type=jnp.float32)

    @pl.when(head == 0)
    def _():
        total[...] = term

    @pl.when(head > 0)
    def _():
        total[...] += term

    @pl.when(head == pl.num_programs(0) - 1)
    def _():
        width = o_ref.shape[2]
        for z in range(o_ref.shape[0]):
            o_ref[z] = total[:, z * width : (z + 1) * width].astype(jnp.bfloat16)


def attend(meta, queries, kvs, out_weight, shards, docs, stripes):
    rows, head_width = queries.shape
    plane = kvs[0].shape[0]
    size = rows // stripes
    heads = head_width // HD
    operands, specs = [], []
    for kv in kvs:
        kv = kv.reshape(plane, 2, stripes, size, head_width)
        for which in range(2):
            operands.append(kv)
            specs.append(
                pl.BlockSpec((plane, None, stripes, size, HD), lambda h, m, which=which: (0, which, 0, 0, h))
            )
    width = out_weight.shape[1]
    operands.append(out_weight)
    specs.append(pl.BlockSpec((HD, width), lambda h, m: (h, 0)))
    pairs = rows * plane * rows * len(kvs)
    return pl.pallas_call(
        functools.partial(attend_kernel, docs, (len(kvs) - 1) * stripes),
        grid_spec=pltpu.PrefetchScalarGridSpec(
            num_scalar_prefetch=1,
            grid=(heads,),
            in_specs=[pl.BlockSpec((rows, HD), lambda h, m: (0, h))] + specs,
            out_specs=pl.BlockSpec((shards, rows, width // shards), lambda h, m: (0, 0, 0)),
            scratch_shapes=[pltpu.VMEM((rows, width), jnp.float32)],
        ),
        out_shape=jax.ShapeDtypeStruct((shards, rows, width // shards), jnp.bfloat16),
        compiler_params=pltpu.CompilerParams(vmem_limit_bytes=VMEM_LIMIT),
        cost_estimate=pl.CostEstimate(
            flops=4 * pairs * head_width, bytes_accessed=4 * kvs[0].size, transcendentals=pairs * heads
        ),
        name="attend",
    )(meta, queries, *operands)


def line_copy(src, dst, send_sem, recv_sem, to):
    return pltpu.make_async_remote_copy(
        src_ref=src,
        dst_ref=dst,
        send_sem=send_sem,
        recv_sem=recv_sem,
        device_id=to,
        device_id_type=pl.DeviceIdType.MESH,
    )


def block_kernel(
    docs, meta_ref, x_ref, w_hbm, wo_hbm, o_ref,
    w, wo, xg, normed, query, kv, num, den, context, terms, from_right, from_left, final,
    w_sem, a_send, a_recv, g_send, g_recv, r_send, r_recv,
):
    shards, rows, width = xg.shape
    stripes, plane, _, size, head_width = kv.shape
    heads = head_width // HD
    period = plane * size
    last = shards - 1
    x, place, z = lax.axis_index("dp"), lax.axis_index("ctx"), lax.axis_index("tensor")
    y, core = place // 2, lax.rem(place, 2)

    def block(flip_x, flip_y, flip_core):
        return (x ^ flip_x) * 4 + (y ^ flip_y) * 2 + (core ^ flip_core)

    def device(flip_x, flip_y, flip_core):
        return {"dp": x ^ flip_x, "ctx": (y ^ flip_y) * 2 + (core ^ flip_core)}

    me = block(0, 0, 0)
    sibling, across_x, across_y = device(0, 0, 1), device(1, 0, 0), device(0, 1, 0)
    left, right = {"tensor": z - 1}, {"tensor": z + 1}

    loads = [pltpu.make_async_copy(w_hbm.at[p], w.at[p], w_sem.at[p]) for p in range(3)]
    loads.append(pltpu.make_async_copy(wo_hbm, wo, w_sem.at[3]))
    for which in (1, 2, 0, 3):
        loads[which].start()

    barrier = pltpu.get_barrier_semaphore()
    for target in (sibling, across_x, across_y):
        pl.semaphore_signal(barrier, inc=1, device_id=target, device_id_type=pl.DeviceIdType.MESH)

    @pl.when(z > 0)
    def _():
        pl.semaphore_signal(barrier, inc=1, device_id=left, device_id_type=pl.DeviceIdType.MESH)

    @pl.when(z < last)
    def _():
        pl.semaphore_signal(barrier, inc=1, device_id=right, device_id_type=pl.DeviceIdType.MESH)

    pl.semaphore_wait(barrier, 3 + jnp.where(z > 0, 1, 0) + jnp.where(z < last, 1, 0))

    def rows_of(s):
        return pl.ds(s * size, size)

    def feature_copy(s, way, hop):
        origin = z + hop if way == 0 else z - hop
        piece = xg.at[origin, rows_of(s)]
        source = x_ref.at[rows_of(s)] if hop == 0 else piece
        return line_copy(source, piece, a_send.at[way, s, hop], a_recv.at[way, s, hop], left if way == 0 else right)

    def feature_sent(way, hop):
        return (z > 0) & (z + hop <= last) if way == 0 else (z < last) & (z - hop >= 0)

    def feature_first(s):
        for way in range(2):

            @pl.when(feature_sent(way, 0))
            def _():
                feature_copy(s, way, 0).start()

    def feature_hop(s, hop):
        for way in range(2):

            @pl.when((z + hop <= last) if way == 0 else (z - hop >= 0))
            def _():
                origin = z + hop if way == 0 else z - hop
                piece = xg.at[origin, rows_of(s)]
                line_copy(
                    piece, piece, a_send.at[way, s, hop - 1], a_recv.at[way, s, hop - 1], left if way == 0 else right
                ).wait_recv()

            if hop < last:

                @pl.when(feature_sent(way, hop))
                def _():
                    feature_copy(s, way, hop).start()

    def feature_end():
        for s in range(stripes):
            for way in range(2):
                for hop in range(last):

                    @pl.when(feature_sent(way, hop))
                    def _():
                        feature_copy(s, way, hop).wait_send()

    first = core == 0
    onward = jnp.where(first, block(0, 1, 0), block(1, 0, 0))
    onward_device = {
        "dp": jnp.where(first, x ^ 1, x),
        "ctx": jnp.where(first, place, (y ^ 1) * 2 + core),
    }
    sent = []

    def kv_send(s, origin, route, target):
        copy = line_copy(kv.at[s, origin], kv.at[s, origin], g_send.at[s, route], g_recv.at[s, route], target)
        copy.start()
        sent.append(copy)

    def kv_arrive(s, origin, route):
        line_copy(
            kv.at[s, origin], kv.at[s, origin], g_send.at[s, route], g_recv.at[s, route], sibling
        ).wait_recv()

    def kv_own(s):
        kv_send(s, me, 1, across_x)
        kv_send(s, me, 2, across_y)
        kv_send(s, me, 0, sibling)

    def kv_near(s):
        kv_arrive(s, block(1, 0, 0), 1)
        kv_arrive(s, block(0, 1, 0), 2)
        kv_send(s, onward, 3, onward_device)
        kv_send(s, block(1, 0, 0), 4, sibling)
        kv_send(s, block(0, 1, 0), 5, sibling)

    def kv_far(s):
        kv_arrive(s, block(1, 1, 0), 3)
        kv_send(s, block(1, 1, 0), 6, sibling)

    def kv_all(s):
        kv_arrive(s, block(0, 0, 1), 0)
        kv_arrive(s, block(1, 0, 1), 4)
        kv_arrive(s, block(0, 1, 1), 5)
        kv_arrive(s, block(1, 1, 1), 6)

    def normalize(s):
        total = jnp.zeros((size, 1), jnp.float32)
        for j in range(shards):
            wide = xg[j, rows_of(s)].astype(jnp.float32)
            total = total + jnp.sum(wide * wide, axis=1, keepdims=True)
        factor = lax.rsqrt(total / (shards * width) + norm_epsilon)
        for j in range(shards):
            normed[:, j * width : (j + 1) * width] = (xg[j, rows_of(s)].astype(jnp.float32) * factor).astype(
                jnp.bfloat16
            )

    def head_normed(acc, scale):
        parts = []
        for h in range(heads):
            head = acc[:, h * HD : (h + 1) * HD]
            factor = lax.rsqrt(jnp.mean(head * head, axis=1, keepdims=True) + head_epsilon) * scale
            parts.append((head * factor).astype(jnp.bfloat16))
        return parts

    def part_of(which):
        return jnp.dot(normed[...], w[which], preferred_element_type=jnp.float32)

    def project_kv(s):
        normalize(s)
        if s == 0:
            loads[1].wait()
        for h, value in enumerate(head_normed(part_of(1), 1.0)):
            kv[s, me, 0, :, h * HD : (h + 1) * HD] = value
        if s == 0:
            loads[2].wait()
        kv[s, me, 1] = part_of(2).astype(jnp.bfloat16)

    def project_q(s):
        if s == 0:
            loads[0].wait()
        for h, value in enumerate(head_normed(part_of(0), score_scale)):
            query[rows_of(s), h * HD : (h + 1) * HD] = value

    row = lax.broadcasted_iota(jnp.int32, (size, 1), 0)
    lane = lax.broadcasted_iota(jnp.int32, (1, period), 1)

    def begin_of(s):
        q_index = s * period + me * size + row
        begin = jnp.zeros((size, 1), jnp.int32)
        for d in range(docs):
            begin = jnp.where(q_index >= meta_ref[d], meta_ref[d], begin)
        return begin

    def attend(s, steps):
        begin = begin_of(s)

        def one_head(h, carry):
            at = pl.ds(pl.multiple_of(h * HD, HD), HD)
            lines = query[rows_of(s), at]
            top = jnp.zeros((size, HD), jnp.float32) if steps[0] == 0 else num[s, :, at]
            low = jnp.zeros((size, 1), jnp.float32) if steps[0] == 0 else den[s, :, at][:, :1]
            for t in steps:
                keys = kv[t, :, 0, :, at].reshape(period, HD)
                values = kv[t, :, 1, :, at].reshape(period, HD)
                scores = lax.dot_general(lines, keys, (((1,), (1,)), ((), ())), preferred_element_type=jnp.float32)
                allowed = lane >= begin - t * period
                if t == s:
                    allowed = allowed & (lane <= me * size + row)
                weights = jnp.where(allowed, jnp.exp(scores), 0.0)
                low = low + jnp.sum(weights, axis=1, keepdims=True)
                top = top + jnp.dot(weights.astype(jnp.bfloat16), values, preferred_element_type=jnp.float32)
            if steps[-1] == s:
                context[:, at] = (top / low).astype(jnp.bfloat16)
            else:
                num[s, :, at] = top
                den[s, :, at] = jnp.broadcast_to(low, (size, HD))
            return carry

        lax.fori_loop(0, heads, one_head, 0)

    def early(s):
        if s > 0:
            attend(s, list(range(s)))

    def late(s):
        attend(s, [s])

    def project_out(s):
        if s == 0:
            loads[3].wait()
        for j in range(shards):
            terms[s, j] = jnp.dot(
                context[...], wo[:, j * width : (j + 1) * width], preferred_element_type=jnp.float32
            ).astype(jnp.bfloat16)

    def sum_copy(s, way, d):
        land = from_right if way == 0 else from_left
        return line_copy(
            terms.at[s, d], land.at[s, d], r_send.at[way, s, d], r_recv.at[way, s, d], left if way == 0 else right
        )

    def sum_sent(way, d):
        return (z > d) if way == 0 else (z < d)

    def sum_step(s, way, d):
        inner = (z < last) if way == 0 else (z > 0)
        land = from_right if way == 0 else from_left

        @pl.when(sum_sent(way, d) & inner)
        def _():
            sum_copy(s, way, d).wait_recv()
            terms[s, d] = (terms[s, d].astype(jnp.float32) + land[s, d].astype(jnp.float32)).astype(jnp.bfloat16)

        @pl.when(sum_sent(way, d))
        def _():
            sum_copy(s, way, d).start()

    def order(way, k):
        return k if way == 0 else last - k

    def sum_round(s, k):
        for way in range(2):
            sum_step(s, way, order(way, k))

    def sum_final(s):
        final[...] = terms[s, z].astype(jnp.float32)
        for way in range(2):
            land = from_right if way == 0 else from_left

            @pl.when((z < last) if way == 0 else (z > 0))
            def _():
                line_copy(
                    terms.at[s, z], land.at[s, z], r_send.at[way, s, z], r_recv.at[way, s, z],
                    left if way == 0 else right,
                ).wait_recv()
                final[...] += land[s, z].astype(jnp.float32)

        o_ref[rows_of(s)] = final[...].astype(jnp.bfloat16)

    def sum_end():
        for s in range(stripes):
            for way in range(2):
                for d in range(shards):

                    @pl.when(sum_sent(way, d))
                    def _():
                        sum_copy(s, way, d).wait_send()

    feature_first(0)
    for s in range(stripes):
        xg[z, rows_of(s)] = x_ref[rows_of(s)]
    for hop in range(1, last):
        feature_hop(0, hop)
    feature_first(1)
    feature_hop(0, last)
    for p in range(1, stripes + 1):
        coming = p < stripes
        project_kv(p - 1)
        kv_own(p - 1)
        if coming:
            feature_hop(p, 1)
        project_q(p - 1)
        if p >= 2:
            kv_all(p - 2)
            late(p - 2)
        if coming:
            feature_hop(p, 2)
        if p >= 2:
            project_out(p - 2)
        kv_near(p - 1)
        if p + 1 < stripes:
            feature_first(p + 1)
        if p >= 2:
            sum_round(p - 2, 0)
        if coming:
            feature_hop(p, last)
        early(p - 1)
        kv_far(p - 1)
        if p >= 2:
            for k in range(1, last):
                sum_round(p - 2, k)
            sum_final(p - 2)
    final_stripe = stripes - 1
    kv_all(final_stripe)
    late(final_stripe)
    project_out(final_stripe)
    for k in range(last):
        sum_round(final_stripe, k)
    sum_final(final_stripe)
    feature_end()
    for copy in sent:
        copy.wait_send()
    sum_end()


def block(meta, packed, weight, out_weight, docs, shards, stripes, plane, call):
    rows, width = packed.shape
    head_width = weight.shape[2]
    full = out_weight.shape[1]
    size = rows // stripes
    sixteen = jnp.bfloat16
    dma = pltpu.SemaphoreType.DMA
    return pl.pallas_call(
        functools.partial(block_kernel, docs),
        in_specs=[
            pl.BlockSpec(memory_space=pltpu.SMEM),
            pl.BlockSpec(memory_space=pltpu.VMEM),
            pl.BlockSpec(memory_space=pl.ANY),
            pl.BlockSpec(memory_space=pl.ANY),
        ],
        out_specs=pl.BlockSpec(memory_space=pltpu.VMEM),
        out_shape=jax.ShapeDtypeStruct((rows, width), sixteen),
        scratch_shapes=[
            pltpu.VMEM(weight.shape, sixteen),
            pltpu.VMEM(out_weight.shape, sixteen),
            pltpu.VMEM((shards, rows, width), sixteen),
            pltpu.VMEM((size, full), sixteen),
            pltpu.VMEM((rows, head_width), sixteen),
            pltpu.VMEM((stripes, plane, 2, size, head_width), sixteen),
            pltpu.VMEM((stripes, size, head_width), jnp.float32),
            pltpu.VMEM((stripes, size, head_width), jnp.float32),
            pltpu.VMEM((size, head_width), sixteen),
            pltpu.VMEM((stripes, shards, size, width), sixteen),
            pltpu.VMEM((stripes, shards, size, width), sixteen),
            pltpu.VMEM((stripes, shards, size, width), sixteen),
            pltpu.VMEM((size, width), jnp.float32),
            dma((4,)),
            dma((2, stripes, shards)),
            dma((2, stripes, shards)),
            dma((stripes, 7)),
            dma((stripes, 7)),
            dma((2, stripes, shards)),
            dma((2, stripes, shards)),
        ],
        compiler_params=pltpu.CompilerParams(
            collective_id=call, has_side_effects=True, vmem_limit_bytes=VMEM_LIMIT
        ),
        cost_estimate=pl.CostEstimate(flops=10_000_000_000, bytes_accessed=100_000_000, transcendentals=0),
        name="block",
    )(meta, packed, weight, out_weight)


def per_device(hidden, depth, qkv_weight, out_weight):
    tokens = hidden[0]
    local_len = tokens.shape[0]
    docs = lax.axis_size("dp")
    ctx_count = lax.axis_size("ctx")
    shards = lax.axis_size("tensor")
    plane = docs * ctx_count
    me = lax.axis_index("dp") * ctx_count + lax.axis_index("ctx")
    size = CAP // plane
    stripes = ACT_DEV // size

    active = depth[0] >= RECURSION
    ones = active.astype(jnp.int32)
    counts = lax.all_gather(jnp.sum(ones)[None], PLANE, axis=0, tiled=True)
    ends = jnp.cumsum(counts)
    starts = ends - counts
    rank = jnp.cumsum(ones) - 1
    slot = jnp.where(active, lax.rem(starts[me] + rank, CAP), -1)
    onehot = (jnp.arange(CAP, dtype=jnp.int32)[:, None] == slot[None, :]).astype(jnp.bfloat16)
    dealt = jnp.dot(onehot, tokens, preferred_element_type=jnp.float32).astype(jnp.bfloat16)
    received = lax.all_to_all(dealt.reshape(plane, size, -1), PLANE, 0, 0)

    index = (
        jnp.arange(stripes, dtype=jnp.int32)[:, None] * CAP
        + me * size
        + jnp.arange(size, dtype=jnp.int32)[None, :]
    )
    owned = (index[None] >= starts[:, None, None]) & (index[None] < ends[:, None, None])
    zero = jnp.zeros((), jnp.bfloat16)
    packed = jnp.where(owned[0][:, :, None], received[0][None], zero)
    for b in range(1, plane):
        packed = jnp.where(owned[b][:, :, None], received[b][None], packed)
    packed = packed.reshape(ACT_DEV, -1)

    chunks = 2
    chunk_stripes = stripes // chunks
    chunk_rows = ACT_DEV // chunks
    weight = jnp.transpose(qkv_weight, (1, 0, 2))
    meta = jnp.concatenate([starts[::ctx_count], me[None]]).astype(jnp.int32)
    fast = (docs, ctx_count) == (2, 4) and stripes >= 2 and shards >= 2
    rows_all = [] if fast else [
        lax.all_gather(packed[c * chunk_rows : (c + 1) * chunk_rows], "tensor", axis=0) for c in range(chunks)
    ]
    kvs, backs = [], []
    for c in range(0 if fast else chunks):
        queries, kv = project(rows_all[c], weight)
        kvs.append(gather_plane(kv, c))
        terms = attend(meta, queries, kvs, out_weight, shards, docs, chunk_stripes)
        backs.append(lax.psum_scatter(terms, "tensor", scatter_dimension=0))
    if fast:
        rows_back = block(meta, packed, weight, out_weight, docs, shards, stripes, plane, 2)
    else:
        rows_back = jnp.concatenate(backs, axis=0)

    rows_back = rows_back.reshape(stripes, size, -1)
    returned = jnp.where(owned[:, 0][:, :, None], rows_back[0][None], zero)
    for k in range(1, stripes):
        returned = jnp.where(owned[:, k][:, :, None], rows_back[k][None], returned)
    landed = lax.all_to_all(returned, PLANE, 0, 0).reshape(CAP, -1)
    spread = (slot[:, None] == jnp.arange(CAP, dtype=jnp.int32)[None, :]).astype(jnp.bfloat16)
    update = jnp.dot(spread, landed, preferred_element_type=jnp.float32).astype(jnp.bfloat16)
    return update[None]


def solution(mesh):
    placed = (P("dp", "ctx", "tensor"), P("dp", "ctx"), P(None, None, "tensor"), P("tensor", None))
    return jax.shard_map(
        per_device, mesh=mesh, in_specs=placed, out_specs=P("dp", "ctx", "tensor"), check_vma=False
    )
```

```python
import functools

import jax
import jax.numpy as jnp
from jax import lax
from jax.experimental import pallas as pl
from jax.experimental.pallas import tpu as pltpu
from jax.sharding import PartitionSpec as P

HD = 128
RECURSION = 3
CAP = 1024
ACT_DEV = 512

score_scale = 0.25
norm_epsilon = 1e-05
head_epsilon = 1e-06
VMEM_LIMIT = 60 * 1024 * 1024
PLANE = ("dp", "ctx")


def project_kernel(x_ref, w_ref, q_ref, kv_ref, normed):
    part = pl.program_id(0)
    shards, rows, width = x_ref.shape

    @pl.when(part == 0)
    def _():
        total = jnp.zeros((rows, 1), jnp.float32)
        for z in range(shards):
            wide = x_ref[z].astype(jnp.float32)
            total = total + jnp.sum(wide * wide, axis=1, keepdims=True)
        factor = lax.rsqrt(total / (shards * width) + norm_epsilon)
        for z in range(shards):
            normed[z] = (x_ref[z].astype(jnp.float32) * factor).astype(jnp.bfloat16)

    acc = jnp.dot(normed[0], w_ref[0, :width], preferred_element_type=jnp.float32)
    for z in range(1, shards):
        acc = acc + jnp.dot(normed[z], w_ref[0, z * width : (z + 1) * width], preferred_element_type=jnp.float32)
    heads = acc.shape[1] // HD

    def head_normed(scale):
        parts = []
        for h in range(heads):
            head = acc[:, h * HD : (h + 1) * HD]
            factor = lax.rsqrt(jnp.mean(head * head, axis=1, keepdims=True) + head_epsilon) * scale
            parts.append((head * factor).astype(jnp.bfloat16))
        return parts

    @pl.when(part == 0)
    def _():
        for h, value in enumerate(head_normed(score_scale)):
            q_ref[:, h * HD : (h + 1) * HD] = value

    @pl.when(part == 1)
    def _():
        for h, value in enumerate(head_normed(1.0)):
            kv_ref[0, :, h * HD : (h + 1) * HD] = value

    @pl.when(part == 2)
    def _():
        kv_ref[0] = acc.astype(jnp.bfloat16)


def project(rows_all, weight):
    shards, rows, width = rows_all.shape
    head_width = weight.shape[2]
    flops = 2 * rows * shards * width * 3 * head_width
    return pl.pallas_call(
        project_kernel,
        grid=(3,),
        out_shape=[
            jax.ShapeDtypeStruct((rows, head_width), jnp.bfloat16),
            jax.ShapeDtypeStruct((2, rows, head_width), jnp.bfloat16),
        ],
        in_specs=[
            pl.BlockSpec((shards, rows, width), lambda p: (0, 0, 0)),
            pl.BlockSpec((1, shards * width, head_width), lambda p: (p, 0, 0)),
        ],
        out_specs=[
            pl.BlockSpec((rows, head_width), lambda p: (0, 0)),
            pl.BlockSpec((1, rows, head_width), lambda p: (jnp.maximum(p - 1, 0), 0, 0)),
        ],
        scratch_shapes=[pltpu.VMEM((shards, rows, width), jnp.bfloat16)],
        compiler_params=pltpu.CompilerParams(vmem_limit_bytes=VMEM_LIMIT),
        cost_estimate=pl.CostEstimate(flops=flops, bytes_accessed=2 * weight.size, transcendentals=0),
        name="project",
    )(rows_all, weight)


def attend_kernel(docs, base, meta_ref, q_ref, *refs):
    w_ref, o_ref, total = refs[-3:]
    pairs = [(refs[i], refs[i + 1]) for i in range(0, len(refs) - 3, 2)]
    head = pl.program_id(0)
    plane, stripes, size, _ = refs[0].shape
    period = plane * size
    rows = stripes * size
    me = meta_ref[docs]
    row = lax.broadcasted_iota(jnp.int32, (rows, 1), 0)
    q_index = (base + row // size) * period + me * size + lax.rem(row, size)
    begin = jnp.zeros((rows, 1), jnp.int32)
    for d in range(docs):
        begin = jnp.where(q_index >= meta_ref[d], meta_ref[d], begin)
    lane = lax.broadcasted_iota(jnp.int32, (1, period), 1)
    query = q_ref[...]
    num = jnp.zeros((rows, HD), jnp.float32)
    den = jnp.zeros((rows, 1), jnp.float32)
    at = 0
    for k_ref, v_ref in pairs:
        for k in range(stripes):
            keys = k_ref[:, k].reshape(period, HD)
            values = v_ref[:, k].reshape(period, HD)
            scores = lax.dot_general(query, keys, (((1,), (1,)), ((), ())), preferred_element_type=jnp.float32)
            allowed = lane >= begin - at * period
            if at >= base:
                allowed = allowed & (lane <= q_index - at * period)
            weights = jnp.where(allowed, jnp.exp(scores), 0.0)
            den = den + jnp.sum(weights, axis=1, keepdims=True)
            num = num + jnp.dot(weights.astype(jnp.bfloat16), values, preferred_element_type=jnp.float32)
            at += 1
    context = (num / den).astype(jnp.bfloat16)
    term = jnp.dot(context, w_ref[...], preferred_element_type=jnp.float32)

    @pl.when(head == 0)
    def _():
        total[...] = term

    @pl.when(head > 0)
    def _():
        total[...] += term

    @pl.when(head == pl.num_programs(0) - 1)
    def _():
        width = o_ref.shape[2]
        for z in range(o_ref.shape[0]):
            o_ref[z] = total[:, z * width : (z + 1) * width].astype(jnp.bfloat16)


def attend(meta, queries, kvs, out_weight, shards, docs, stripes):
    rows, head_width = queries.shape
    plane = kvs[0].shape[0]
    size = rows // stripes
    heads = head_width // HD
    operands, specs = [], []
    for kv in kvs:
        kv = kv.reshape(plane, 2, stripes, size, head_width)
        for which in range(2):
            operands.append(kv)
            specs.append(
                pl.BlockSpec((plane, None, stripes, size, HD), lambda h, m, which=which: (0, which, 0, 0, h))
            )
    width = out_weight.shape[1]
    operands.append(out_weight)
    specs.append(pl.BlockSpec((HD, width), lambda h, m: (h, 0)))
    pairs = rows * plane * rows * len(kvs)
    return pl.pallas_call(
        functools.partial(attend_kernel, docs, (len(kvs) - 1) * stripes),
        grid_spec=pltpu.PrefetchScalarGridSpec(
            num_scalar_prefetch=1,
            grid=(heads,),
            in_specs=[pl.BlockSpec((rows, HD), lambda h, m: (0, h))] + specs,
            out_specs=pl.BlockSpec((shards, rows, width // shards), lambda h, m: (0, 0, 0)),
            scratch_shapes=[pltpu.VMEM((rows, width), jnp.float32)],
        ),
        out_shape=jax.ShapeDtypeStruct((shards, rows, width // shards), jnp.bfloat16),
        compiler_params=pltpu.CompilerParams(vmem_limit_bytes=VMEM_LIMIT),
        cost_estimate=pl.CostEstimate(
            flops=4 * pairs * head_width, bytes_accessed=4 * kvs[0].size, transcendentals=pairs * heads
        ),
        name="attend",
    )(meta, queries, *operands)


def line_copy(src, dst, send_sem, recv_sem, to):
    return pltpu.make_async_remote_copy(
        src_ref=src,
        dst_ref=dst,
        send_sem=send_sem,
        recv_sem=recv_sem,
        device_id=to,
        device_id_type=pl.DeviceIdType.MESH,
    )


def block_kernel(
    docs, first_meta, meta_ref, deal_ref, w_hbm, wo_hbm, landed_ref,
    received, x_ref, o_ref, returned, w, wo, xg, normed, query, kv, num, den, context, terms, from_right, from_left, final,
    w_sem, a_send, a_recv, g_send, g_recv, r_send, r_recv, d_send, d_recv, b_send, b_recv,
):
    shards, rows, width = xg.shape
    stripes, plane, _, size, head_width = kv.shape
    heads = head_width // HD
    period = plane * size
    last = shards - 1
    row = lax.broadcasted_iota(jnp.int32, (size, 1), 0)
    x, place, z = lax.axis_index("dp"), lax.axis_index("ctx"), lax.axis_index("tensor")
    y, core = place // 2, lax.rem(place, 2)

    def block(flip_x, flip_y, flip_core):
        return (x ^ flip_x) * 4 + (y ^ flip_y) * 2 + (core ^ flip_core)

    def device(flip_x, flip_y, flip_core):
        return {"dp": x ^ flip_x, "ctx": (y ^ flip_y) * 2 + (core ^ flip_core)}

    def peer(flip):
        flips = flip // 4, (flip // 2) % 2, flip % 2
        return block(*flips), device(*flips)

    me = block(0, 0, 0)
    sibling, across_x, across_y = device(0, 0, 1), device(1, 0, 0), device(0, 1, 0)
    left, right = {"tensor": z - 1}, {"tensor": z + 1}

    loads = [pltpu.make_async_copy(w_hbm.at[p], w.at[p], w_sem.at[p]) for p in range(3)]
    loads.append(pltpu.make_async_copy(wo_hbm, wo, w_sem.at[3]))
    for which in (1, 2, 0, 3):
        loads[which].start()

    barrier = pltpu.get_barrier_semaphore()
    for flip in range(1, plane):
        pl.semaphore_signal(barrier, inc=1, device_id=peer(flip)[1], device_id_type=pl.DeviceIdType.MESH)

    @pl.when(z > 0)
    def _():
        pl.semaphore_signal(barrier, inc=1, device_id=left, device_id_type=pl.DeviceIdType.MESH)

    @pl.when(z < last)
    def _():
        pl.semaphore_signal(barrier, inc=1, device_id=right, device_id_type=pl.DeviceIdType.MESH)

    pl.semaphore_wait(barrier, plane - 1 + jnp.where(z > 0, 1, 0) + jnp.where(z < last, 1, 0))

    def rows_of(s):
        return pl.ds(s * size, size)

    def deal_copy(flip):
        other, target = peer(flip)
        return line_copy(deal_ref.at[other], received.at[me], d_send.at[flip], d_recv.at[flip], target)

    def back_copy(flip):
        other, target = peer(flip)
        return line_copy(returned.at[other], landed_ref.at[me], b_send.at[flip], b_recv.at[flip], target)

    far_first = (6, 7, 4, 5, 2, 3, 1)

    def owned(b, s):
        index = s * period + me * size + row
        return (index >= meta_ref[first_meta + b]) & (index < meta_ref[first_meta + b + 1])

    def deal():
        for flip in far_first:
            deal_copy(flip).start()
        received[me] = deal_ref[me]
        for flip in far_first:
            other, target = peer(flip)
            line_copy(deal_ref.at[other], received.at[other], d_send.at[flip], d_recv.at[flip], target).wait_recv()
        for s in range(stripes):
            picked = jnp.zeros((size, width), jnp.float32)
            for b in range(plane):
                picked = jnp.where(owned(b, s), received[b].astype(jnp.float32), picked)
            x_ref[rows_of(s)] = picked.astype(jnp.bfloat16)

    def give_back():
        for b in range(plane):
            picked = jnp.zeros((size, width), jnp.float32)
            for s in range(stripes):
                picked = jnp.where(owned(b, s), o_ref[rows_of(s)].astype(jnp.float32), picked)
            returned[b] = picked.astype(jnp.bfloat16)
        for flip in far_first:
            back_copy(flip).start()
        landed_ref[me] = returned[me]
        for flip in far_first:
            other, target = peer(flip)
            line_copy(returned.at[other], landed_ref.at[other], b_send.at[flip], b_recv.at[flip], target).wait_recv()
        for flip in far_first:
            deal_copy(flip).wait_send()
            back_copy(flip).wait_send()

    def feature_copy(s, way, hop):
        origin = z + hop if way == 0 else z - hop
        piece = xg.at[origin, rows_of(s)]
        source = x_ref.at[rows_of(s)] if hop == 0 else piece
        return line_copy(source, piece, a_send.at[way, s, hop], a_recv.at[way, s, hop], left if way == 0 else right)

    def feature_sent(way, hop):
        return (z > 0) & (z + hop <= last) if way == 0 else (z < last) & (z - hop >= 0)

    def feature_first(s):
        for way in range(2):

            @pl.when(feature_sent(way, 0))
            def _():
                feature_copy(s, way, 0).start()

    def feature_hop(s, hop):
        for way in range(2):

            @pl.when((z + hop <= last) if way == 0 else (z - hop >= 0))
            def _():
                origin = z + hop if way == 0 else z - hop
                piece = xg.at[origin, rows_of(s)]
                line_copy(
                    piece, piece, a_send.at[way, s, hop - 1], a_recv.at[way, s, hop - 1], left if way == 0 else right
                ).wait_recv()

            if hop < last:

                @pl.when(feature_sent(way, hop))
                def _():
                    feature_copy(s, way, hop).start()

    def feature_end():
        for s in range(stripes):
            for way in range(2):
                for hop in range(last):

                    @pl.when(feature_sent(way, hop))
                    def _():
                        feature_copy(s, way, hop).wait_send()

    first = core == 0
    onward = jnp.where(first, block(0, 1, 0), block(1, 0, 0))
    onward_device = {
        "dp": jnp.where(first, x ^ 1, x),
        "ctx": jnp.where(first, place, (y ^ 1) * 2 + core),
    }
    sent = []

    def kv_send(s, origin, route, target):
        copy = line_copy(kv.at[s, origin], kv.at[s, origin], g_send.at[s, route], g_recv.at[s, route], target)
        copy.start()
        sent.append(copy)

    def kv_arrive(s, origin, route):
        line_copy(
            kv.at[s, origin], kv.at[s, origin], g_send.at[s, route], g_recv.at[s, route], sibling
        ).wait_recv()

    def kv_own(s):
        kv_send(s, me, 1, across_x)
        kv_send(s, me, 2, across_y)
        kv_send(s, me, 0, sibling)

    def kv_near(s):
        kv_arrive(s, block(1, 0, 0), 1)
        kv_arrive(s, block(0, 1, 0), 2)
        kv_send(s, onward, 3, onward_device)
        kv_send(s, block(1, 0, 0), 4, sibling)
        kv_send(s, block(0, 1, 0), 5, sibling)

    def kv_far(s):
        kv_arrive(s, block(1, 1, 0), 3)
        kv_send(s, block(1, 1, 0), 6, sibling)

    def kv_all(s):
        kv_arrive(s, block(0, 0, 1), 0)
        kv_arrive(s, block(1, 0, 1), 4)
        kv_arrive(s, block(0, 1, 1), 5)
        kv_arrive(s, block(1, 1, 1), 6)

    def normalize(s):
        total = jnp.zeros((size, 1), jnp.float32)
        for j in range(shards):
            wide = xg[j, rows_of(s)].astype(jnp.float32)
            total = total + jnp.sum(wide * wide, axis=1, keepdims=True)
        factor = lax.rsqrt(total / (shards * width) + norm_epsilon)
        for j in range(shards):
            normed[:, j * width : (j + 1) * width] = (xg[j, rows_of(s)].astype(jnp.float32) * factor).astype(
                jnp.bfloat16
            )

    def head_normed(acc, scale):
        parts = []
        for h in range(heads):
            head = acc[:, h * HD : (h + 1) * HD]
            factor = lax.rsqrt(jnp.mean(head * head, axis=1, keepdims=True) + head_epsilon) * scale
            parts.append((head * factor).astype(jnp.bfloat16))
        return parts

    def part_of(which):
        return jnp.dot(normed[...], w[which], preferred_element_type=jnp.float32)

    def project_kv(s):
        normalize(s)
        if s == 0:
            loads[1].wait()
        for h, value in enumerate(head_normed(part_of(1), 1.0)):
            kv[s, me, 0, :, h * HD : (h + 1) * HD] = value
        if s == 0:
            loads[2].wait()
        kv[s, me, 1] = part_of(2).astype(jnp.bfloat16)

    def project_q(s):
        if s == 0:
            loads[0].wait()
        for h, value in enumerate(head_normed(part_of(0), score_scale)):
            query[rows_of(s), h * HD : (h + 1) * HD] = value

    lane = lax.broadcasted_iota(jnp.int32, (1, period), 1)

    def begin_of(s):
        q_index = s * period + me * size + row
        begin = jnp.zeros((size, 1), jnp.int32)
        for d in range(docs):
            at = first_meta + d * (plane // docs)
            begin = jnp.where(q_index >= meta_ref[at], meta_ref[at], begin)
        return begin

    def attend(s, steps):
        begin = begin_of(s)

        def one_head(h, carry):
            at = pl.ds(pl.multiple_of(h * HD, HD), HD)
            lines = query[rows_of(s), at]
            top = jnp.zeros((size, HD), jnp.float32) if steps[0] == 0 else num[s, :, at]
            low = jnp.zeros((size, 1), jnp.float32) if steps[0] == 0 else den[s, :, at][:, :1]
            for t in steps:
                keys = kv[t, :, 0, :, at].reshape(period, HD)
                values = kv[t, :, 1, :, at].reshape(period, HD)
                scores = lax.dot_general(lines, keys, (((1,), (1,)), ((), ())), preferred_element_type=jnp.float32)
                allowed = lane >= begin - t * period
                if t == s:
                    allowed = allowed & (lane <= me * size + row)
                weights = jnp.where(allowed, jnp.exp(scores), 0.0)
                low = low + jnp.sum(weights, axis=1, keepdims=True)
                top = top + jnp.dot(weights.astype(jnp.bfloat16), values, preferred_element_type=jnp.float32)
            if steps[-1] == s:
                context[:, at] = (top / low).astype(jnp.bfloat16)
            else:
                num[s, :, at] = top
                den[s, :, at] = jnp.broadcast_to(low, (size, HD))
            return carry

        lax.fori_loop(0, heads, one_head, 0)

    def early(s):
        if s > 0:
            attend(s, list(range(s)))

    def late(s):
        attend(s, [s])

    def project_out(s):
        if s == 0:
            loads[3].wait()
        for j in range(shards):
            terms[s, j] = jnp.dot(
                context[...], wo[:, j * width : (j + 1) * width], preferred_element_type=jnp.float32
            ).astype(jnp.bfloat16)

    def sum_copy(s, way, d):
        land = from_right if way == 0 else from_left
        return line_copy(
            terms.at[s, d], land.at[s, d], r_send.at[way, s, d], r_recv.at[way, s, d], left if way == 0 else right
        )

    def sum_sent(way, d):
        return (z > d) if way == 0 else (z < d)

    def sum_first(s):
        for way in range(2):
            for k in range(last):

                @pl.when(z == (last if way == 0 else 0))
                def _():
                    sum_copy(s, way, k if way == 0 else last - k).start()

    def sum_round(s, r):
        for way in range(2):
            land = from_right if way == 0 else from_left
            k = r - last + z if way == 0 else r - z
            d = k if way == 0 else last - k

            @pl.when((k >= 0) & ((z < last) if way == 0 else (z > 0)))
            def _():
                sum_copy(s, way, d).wait_recv()
                terms[s, d] = (terms[s, d].astype(jnp.float32) + land[s, d].astype(jnp.float32)).astype(jnp.bfloat16)
                sum_copy(s, way, d).start()

    def sum_final(s):
        final[...] = terms[s, z].astype(jnp.float32)
        for way in range(2):
            land = from_right if way == 0 else from_left

            @pl.when((z < last) if way == 0 else (z > 0))
            def _():
                sum_copy(s, way, z).wait_recv()
                final[...] += land[s, z].astype(jnp.float32)

        o_ref[rows_of(s)] = final[...].astype(jnp.bfloat16)

    def sum_end():
        for s in range(stripes):
            for way in range(2):
                for d in range(shards):

                    @pl.when(sum_sent(way, d))
                    def _():
                        sum_copy(s, way, d).wait_send()

    deal()
    feature_first(0)
    for s in range(stripes):
        xg[z, rows_of(s)] = x_ref[rows_of(s)]
    feature_hop(0, 1)
    feature_first(1)
    for hop in range(2, last + 1):
        feature_hop(0, hop)
    for p in range(stripes + 2):
        here, coming = p < stripes, p + 1 < stripes
        before, older, oldest = 0 <= p - 1 < stripes, 0 <= p - 2 < stripes, 0 <= p - 3 < stripes
        if here:
            project_kv(p)
            kv_own(p)
        if before:
            kv_near(p - 1)
        if here:
            project_q(p)
        if oldest:
            sum_final(p - 3)
        if coming:
            feature_hop(p + 1, 1)
            if p + 2 < stripes:
                feature_first(p + 2)
        if before:
            kv_far(p - 1)
        if older:
            sum_round(p - 2, 1)
        if before:
            kv_all(p - 1)
        if coming:
            feature_hop(p + 1, 2)
        if before:
            late(p - 1)
            project_out(p - 1)
            sum_first(p - 1)
        if older:
            for r in range(2, last):
                sum_round(p - 2, r)
        if here:
            early(p)
        if coming:
            for hop in range(3, last + 1):
                feature_hop(p + 1, hop)
    sum_final(stripes - 1)
    give_back()
    feature_end()
    for copy in sent:
        copy.wait_send()
    sum_end()


def block(meta, first_meta, dealt, weight, out_weight, docs, shards, stripes, call):
    plane, size, width = dealt.shape
    rows = stripes * size
    head_width = weight.shape[2]
    full = out_weight.shape[1]
    sixteen = jnp.bfloat16
    dma = pltpu.SemaphoreType.DMA
    return pl.pallas_call(
        functools.partial(block_kernel, docs, first_meta),
        in_specs=[
            pl.BlockSpec(memory_space=pltpu.SMEM),
            pl.BlockSpec(memory_space=pltpu.VMEM),
            pl.BlockSpec(memory_space=pl.ANY),
            pl.BlockSpec(memory_space=pl.ANY),
        ],
        out_specs=pl.BlockSpec(memory_space=pltpu.VMEM),
        out_shape=jax.ShapeDtypeStruct((plane, size, width), sixteen),
        scratch_shapes=[
            pltpu.VMEM((plane, size, width), sixteen),
            pltpu.VMEM((rows, width), sixteen),
            pltpu.VMEM((rows, width), sixteen),
            pltpu.VMEM((plane, size, width), sixteen),
            pltpu.VMEM(weight.shape, sixteen),
            pltpu.VMEM(out_weight.shape, sixteen),
            pltpu.VMEM((shards, rows, width), sixteen),
            pltpu.VMEM((size, full), sixteen),
            pltpu.VMEM((rows, head_width), sixteen),
            pltpu.VMEM((stripes, plane, 2, size, head_width), sixteen),
            pltpu.VMEM((stripes, size, head_width), jnp.float32),
            pltpu.VMEM((stripes, size, head_width), jnp.float32),
            pltpu.VMEM((size, head_width), sixteen),
            pltpu.VMEM((stripes, shards, size, width), sixteen),
            pltpu.VMEM((stripes, shards, size, width), sixteen),
            pltpu.VMEM((stripes, shards, size, width), sixteen),
            pltpu.VMEM((size, width), jnp.float32),
            dma((4,)),
            dma((2, stripes, shards)),
            dma((2, stripes, shards)),
            dma((stripes, 7)),
            dma((stripes, 7)),
            dma((2, stripes, shards)),
            dma((2, stripes, shards)),
            dma((plane,)),
            dma((plane,)),
            dma((plane,)),
            dma((plane,)),
        ],
        compiler_params=pltpu.CompilerParams(
            collective_id=call, has_side_effects=True, vmem_limit_bytes=VMEM_LIMIT
        ),
        cost_estimate=pl.CostEstimate(flops=10_000_000_000, bytes_accessed=100_000_000, transcendentals=0),
        name="block",
    )(meta, dealt, weight, out_weight)


LINES = 32


def count_kernel(depth_ref, place_ref, info_ref, mine, landed, send_sem, recv_sem):
    plane = landed.shape[0]
    lines, lanes = depth_ref.shape
    ctx_count = lax.axis_size("ctx")
    x, place = lax.axis_index("dp"), lax.axis_index("ctx")
    me = x * ctx_count + place

    def device(flip):
        return {"dp": x ^ (flip // ctx_count), "ctx": place ^ (flip % ctx_count)}

    barrier = pltpu.get_barrier_semaphore()
    for flip in range(1, plane):
        pl.semaphore_signal(barrier, inc=1, device_id=device(flip), device_id_type=pl.DeviceIdType.MESH)
    active = depth_ref[...] >= RECURSION
    ones = jnp.where(active, 1.0, 0.0)
    total = jnp.sum(jnp.sum(ones, axis=1, keepdims=True), axis=0, keepdims=True)
    mine[...] = jnp.broadcast_to(total, mine.shape).astype(jnp.int32)
    pl.semaphore_wait(barrier, plane - 1)

    def copy(flip, slot):
        return line_copy(mine, landed.at[slot], send_sem.at[flip], recv_sem.at[flip], device(flip))

    for flip in range(1, plane):
        copy(flip, me).start()
    landed[me] = mine[...]
    upto = lax.broadcasted_iota(jnp.int32, (lanes, lanes), 0) <= lax.broadcasted_iota(jnp.int32, (lanes, lanes), 1)
    inside = jnp.dot(
        ones.astype(jnp.bfloat16), jnp.where(upto, 1.0, 0.0).astype(jnp.bfloat16), preferred_element_type=jnp.float32
    )
    ahead = lax.broadcasted_iota(jnp.int32, (lines, lines), 1) < lax.broadcasted_iota(jnp.int32, (lines, lines), 0)
    line_total = jnp.broadcast_to(inside[:, lanes - 1 :], (lines, lanes))
    before = jnp.dot(
        jnp.where(ahead, 1.0, 0.0).astype(jnp.bfloat16),
        line_total.astype(jnp.bfloat16),
        preferred_element_type=jnp.float32,
    )
    for flip in range(1, plane):
        copy(flip, me ^ flip).wait_recv()
    start = jnp.zeros((1, lanes), jnp.int32)
    running = jnp.zeros((1, lanes), jnp.int32)
    for b in range(plane):
        info_ref[lines + b : lines + b + 1] = running
        count = landed[b, 0:1]
        start = start + jnp.where(me > b, count, 0)
        running = running + count
    for b in range(plane, info_ref.shape[0] - lines):
        info_ref[lines + b : lines + b + 1] = running
    base = (start & (CAP - 1)) + before.astype(jnp.int32)
    info_ref[:lines] = base
    place_ref[...] = jnp.where(active, base + inside.astype(jnp.int32) - 1, -1)
    for flip in range(1, plane):
        copy(flip, me).wait_send()


def count(depth, plane, call):
    lines = LINES
    lanes = depth.shape[0] // lines
    whole = jnp.int32
    return pl.pallas_call(
        count_kernel,
        in_specs=[pl.BlockSpec(memory_space=pltpu.VMEM)],
        out_specs=[pl.BlockSpec(memory_space=pltpu.VMEM)] * 2,
        out_shape=[
            jax.ShapeDtypeStruct((lines, lanes), whole),
            jax.ShapeDtypeStruct((lines + 16, lanes), whole),
        ],
        scratch_shapes=[
            pltpu.VMEM((8, lanes), whole),
            pltpu.VMEM((plane, 8, lanes), whole),
            pltpu.SemaphoreType.DMA((plane,)),
            pltpu.SemaphoreType.DMA((plane,)),
        ],
        compiler_params=pltpu.CompilerParams(collective_id=call, has_side_effects=True),
        name="count",
    )(depth.reshape(lines, lanes))


ALIGN = 16
GROUP = 2
LOADS = 8


def onehot_of(place_ref, at, floor, window):
    wanted = jnp.concatenate([place_ref[pl.ds(at + i, 1), :] for i in range(GROUP)], axis=1)
    spot = lax.broadcasted_iota(jnp.int32, (window, wanted.shape[1]), 0)
    return jnp.where(spot + floor == wanted, 1.0, 0.0).astype(jnp.bfloat16)


def compact_kernel(info_ref, place_ref, tokens_hbm, out_ref, tokens, buffer, sems):
    lines, lanes = place_ref.shape
    block_rows = GROUP * lanes
    window = block_rows + ALIGN
    chunk = tokens.shape[0] // LOADS
    loads = []
    for i in range(LOADS):
        rows = pl.ds(i * chunk, chunk)
        loads.append(pltpu.make_async_copy(tokens_hbm.at[rows], tokens.at[rows], sems.at[i]))
        loads[-1].start()
    start = info_ref[0]
    edge = lax.broadcasted_iota(jnp.int32, (ALIGN, 1), 0)
    for i in range(lines // GROUP):
        if (i * block_rows) % chunk == 0:
            loads[i * block_rows // chunk].wait()
        base = info_ref[i * GROUP]
        floor = pl.multiple_of(base - lax.rem(base, ALIGN), ALIGN)
        spread = onehot_of(place_ref, i * GROUP, floor, window)
        rows = tokens[i * block_rows : (i + 1) * block_rows]
        found = jnp.dot(spread, rows, preferred_element_type=jnp.float32)
        old = buffer[pl.ds(floor, ALIGN)].astype(jnp.float32)
        seam = jnp.where(edge < base - floor, old, found[:ALIGN])
        buffer[pl.ds(floor, ALIGN)] = seam.astype(jnp.bfloat16)
        buffer[pl.ds(floor + ALIGN, block_rows)] = found[ALIGN:].astype(jnp.bfloat16)
    plane, size, _ = out_ref.shape
    for b in range(plane):
        spot = b * size + lax.broadcasted_iota(jnp.int32, (size, 1), 0)
        low = buffer[b * size : (b + 1) * size].astype(jnp.float32)
        high = buffer[CAP + b * size : CAP + (b + 1) * size].astype(jnp.float32)
        out_ref[b] = jnp.where(spot >= start, low, high).astype(jnp.bfloat16)


def compact(info, places, tokens, plane):
    lines, lanes = places.shape
    width = tokens.shape[1]
    return pl.pallas_call(
        compact_kernel,
        in_specs=[
            pl.BlockSpec(memory_space=pltpu.SMEM),
            pl.BlockSpec(memory_space=pltpu.VMEM),
            pl.BlockSpec(memory_space=pl.ANY),
        ],
        out_specs=pl.BlockSpec(memory_space=pltpu.VMEM),
        out_shape=jax.ShapeDtypeStruct((plane, CAP // plane, width), tokens.dtype),
        scratch_shapes=[
            pltpu.VMEM(tokens.shape, tokens.dtype),
            pltpu.VMEM((2 * CAP + GROUP * lanes + ALIGN, width), tokens.dtype),
            pltpu.SemaphoreType.DMA((LOADS,)),
        ],
        compiler_params=pltpu.CompilerParams(vmem_limit_bytes=VMEM_LIMIT),
        name="compact",
    )(info, places, tokens)


def unpack_kernel(parts, info_ref, place_ref, landed_ref, out_ref, buffer):
    step = pl.program_id(0)
    _, lanes = place_ref.shape
    block_rows = GROUP * lanes
    window = block_rows + ALIGN

    @pl.when(step == 0)
    def _():
        buffer[:CAP] = landed_ref[...]
        buffer[CAP:] = landed_ref[: buffer.shape[0] - CAP]

    for i in range(parts):
        line = (step * parts + i) * GROUP
        base = info_ref[line]
        floor = base - lax.rem(base, ALIGN)
        spread = onehot_of(place_ref, line, floor, window)
        rows = buffer[pl.ds(pl.multiple_of(lax.rem(floor, CAP), ALIGN), window)]
        out_ref[i * block_rows : (i + 1) * block_rows] = lax.dot_general(
            spread, rows, (((0,), (0,)), ((), ())), preferred_element_type=jnp.float32
        ).astype(jnp.bfloat16)


def unpack(info, places, landed, length):
    lines, lanes = places.shape
    width = landed.shape[1]
    steps = 8
    parts = lines // GROUP // steps
    return pl.pallas_call(
        functools.partial(unpack_kernel, parts),
        grid_spec=pltpu.PrefetchScalarGridSpec(
            num_scalar_prefetch=1,
            grid=(steps,),
            in_specs=[
                pl.BlockSpec((lines, lanes), lambda i, m: (0, 0)),
                pl.BlockSpec(landed.shape, lambda i, m: (0, 0)),
            ],
            out_specs=pl.BlockSpec((length // steps, width), lambda i, m: (i, 0)),
            scratch_shapes=[pltpu.VMEM((CAP + GROUP * lanes + ALIGN, width), landed.dtype)],
        ),
        out_shape=jax.ShapeDtypeStruct((length, width), landed.dtype),
        compiler_params=pltpu.CompilerParams(vmem_limit_bytes=VMEM_LIMIT),
        name="unpack",
    )(info, places, landed)


def per_device(hidden, depth, qkv_weight, out_weight):
    tokens = hidden[0]
    local_len = tokens.shape[0]
    docs = lax.axis_size("dp")
    ctx_count = lax.axis_size("ctx")
    shards = lax.axis_size("tensor")
    plane = docs * ctx_count
    me = lax.axis_index("dp") * ctx_count + lax.axis_index("ctx")
    size = CAP // plane
    stripes = ACT_DEV // size

    if (docs, ctx_count) == (2, 4) and local_len % (LINES * 128) == 0 and stripes >= 2 and shards >= 2:
        places, info = count(depth[0], plane, 0)
        info = info[:, 0]
        dealt = compact(info, places, tokens, plane)
        weight = jnp.transpose(qkv_weight, (1, 0, 2))
        landed = block(info, LINES, dealt, weight, out_weight, docs, shards, stripes, 1)
        return unpack(info, places, landed.reshape(CAP, -1), local_len)[None]

    active = depth[0] >= RECURSION
    ones = active.astype(jnp.int32)
    counts = lax.all_gather(jnp.sum(ones)[None], PLANE, axis=0, tiled=True)
    ends = jnp.cumsum(counts)
    starts = ends - counts
    rank = jnp.cumsum(ones) - 1
    slot = jnp.where(active, lax.rem(starts[me] + rank, CAP), -1)
    onehot = (jnp.arange(CAP, dtype=jnp.int32)[:, None] == slot[None, :]).astype(jnp.bfloat16)
    dealt = jnp.dot(onehot, tokens, preferred_element_type=jnp.float32).astype(jnp.bfloat16)
    received = lax.all_to_all(dealt.reshape(plane, size, -1), PLANE, 0, 0)

    index = (
        jnp.arange(stripes, dtype=jnp.int32)[:, None] * CAP
        + me * size
        + jnp.arange(size, dtype=jnp.int32)[None, :]
    )
    owned = (index[None] >= starts[:, None, None]) & (index[None] < ends[:, None, None])
    zero = jnp.zeros((), jnp.bfloat16)
    packed = jnp.where(owned[0][:, :, None], received[0][None], zero)
    for b in range(1, plane):
        packed = jnp.where(owned[b][:, :, None], received[b][None], packed)
    packed = packed.reshape(ACT_DEV, -1)

    chunks = 2
    chunk_stripes = stripes // chunks
    chunk_rows = ACT_DEV // chunks
    weight = jnp.transpose(qkv_weight, (1, 0, 2))
    meta = jnp.concatenate([starts[::ctx_count], me[None]]).astype(jnp.int32)
    rows_all = [
        lax.all_gather(packed[c * chunk_rows : (c + 1) * chunk_rows], "tensor", axis=0) for c in range(chunks)
    ]
    kvs, backs = [], []
    for c in range(chunks):
        queries, kv = project(rows_all[c], weight)
        kvs.append(lax.all_gather(kv, PLANE, axis=0))
        terms = attend(meta, queries, kvs, out_weight, shards, docs, chunk_stripes)
        backs.append(lax.psum_scatter(terms, "tensor", scatter_dimension=0))
    rows_back = jnp.concatenate(backs, axis=0)

    rows_back = rows_back.reshape(stripes, size, -1)
    returned = jnp.where(owned[:, 0][:, :, None], rows_back[0][None], zero)
    for k in range(1, stripes):
        returned = jnp.where(owned[:, k][:, :, None], rows_back[k][None], returned)
    landed = lax.all_to_all(returned, PLANE, 0, 0).reshape(CAP, -1)
    spread = (slot[:, None] == jnp.arange(CAP, dtype=jnp.int32)[None, :]).astype(jnp.bfloat16)
    update = jnp.dot(spread, landed, preferred_element_type=jnp.float32).astype(jnp.bfloat16)
    return update[None]


def solution(mesh):
    placed = (P("dp", "ctx", "tensor"), P("dp", "ctx"), P(None, None, "tensor"), P("tensor", None))
    return jax.shard_map(
        per_device, mesh=mesh, in_specs=placed, out_specs=P("dp", "ctx", "tensor"), check_vma=False
    )
```

```python
import functools

import jax
import jax.numpy as jnp
from jax import lax
from jax.experimental import pallas as pl
from jax.experimental.pallas import tpu as pltpu
from jax.sharding import PartitionSpec as P

HD = 128
RECURSION = 3
CAP = 1024
ACT_DEV = 512

score_scale = 0.25
norm_epsilon = 1e-05
head_epsilon = 1e-06
VMEM_LIMIT = 60 * 1024 * 1024
PLANE = ("dp", "ctx")


def project_kernel(x_ref, w_ref, q_ref, kv_ref, normed):
    part = pl.program_id(0)
    shards, rows, width = x_ref.shape

    @pl.when(part == 0)
    def _():
        total = jnp.zeros((rows, 1), jnp.float32)
        for z in range(shards):
            wide = x_ref[z].astype(jnp.float32)
            total = total + jnp.sum(wide * wide, axis=1, keepdims=True)
        factor = lax.rsqrt(total / (shards * width) + norm_epsilon)
        for z in range(shards):
            normed[z] = (x_ref[z].astype(jnp.float32) * factor).astype(jnp.bfloat16)

    acc = jnp.dot(normed[0], w_ref[0, :width], preferred_element_type=jnp.float32)
    for z in range(1, shards):
        acc = acc + jnp.dot(normed[z], w_ref[0, z * width : (z + 1) * width], preferred_element_type=jnp.float32)
    heads = acc.shape[1] // HD

    def head_normed(scale):
        parts = []
        for h in range(heads):
            head = acc[:, h * HD : (h + 1) * HD]
            factor = lax.rsqrt(jnp.mean(head * head, axis=1, keepdims=True) + head_epsilon) * scale
            parts.append((head * factor).astype(jnp.bfloat16))
        return parts

    @pl.when(part == 0)
    def _():
        for h, value in enumerate(head_normed(score_scale)):
            q_ref[:, h * HD : (h + 1) * HD] = value

    @pl.when(part == 1)
    def _():
        for h, value in enumerate(head_normed(1.0)):
            kv_ref[0, :, h * HD : (h + 1) * HD] = value

    @pl.when(part == 2)
    def _():
        kv_ref[0] = acc.astype(jnp.bfloat16)


def project(rows_all, weight):
    shards, rows, width = rows_all.shape
    head_width = weight.shape[2]
    flops = 2 * rows * shards * width * 3 * head_width
    return pl.pallas_call(
        project_kernel,
        grid=(3,),
        out_shape=[
            jax.ShapeDtypeStruct((rows, head_width), jnp.bfloat16),
            jax.ShapeDtypeStruct((2, rows, head_width), jnp.bfloat16),
        ],
        in_specs=[
            pl.BlockSpec((shards, rows, width), lambda p: (0, 0, 0)),
            pl.BlockSpec((1, shards * width, head_width), lambda p: (p, 0, 0)),
        ],
        out_specs=[
            pl.BlockSpec((rows, head_width), lambda p: (0, 0)),
            pl.BlockSpec((1, rows, head_width), lambda p: (jnp.maximum(p - 1, 0), 0, 0)),
        ],
        scratch_shapes=[pltpu.VMEM((shards, rows, width), jnp.bfloat16)],
        compiler_params=pltpu.CompilerParams(vmem_limit_bytes=VMEM_LIMIT),
        cost_estimate=pl.CostEstimate(flops=flops, bytes_accessed=2 * weight.size, transcendentals=0),
        name="project",
    )(rows_all, weight)


def attend_kernel(docs, base, meta_ref, q_ref, *refs):
    w_ref, o_ref, total = refs[-3:]
    pairs = [(refs[i], refs[i + 1]) for i in range(0, len(refs) - 3, 2)]
    head = pl.program_id(0)
    plane, stripes, size, _ = refs[0].shape
    period = plane * size
    rows = stripes * size
    me = meta_ref[docs]
    row = lax.broadcasted_iota(jnp.int32, (rows, 1), 0)
    q_index = (base + row // size) * period + me * size + lax.rem(row, size)
    begin = jnp.zeros((rows, 1), jnp.int32)
    for d in range(docs):
        begin = jnp.where(q_index >= meta_ref[d], meta_ref[d], begin)
    lane = lax.broadcasted_iota(jnp.int32, (1, period), 1)
    query = q_ref[...]
    num = jnp.zeros((rows, HD), jnp.float32)
    den = jnp.zeros((rows, 1), jnp.float32)
    at = 0
    for k_ref, v_ref in pairs:
        for k in range(stripes):
            keys = k_ref[:, k].reshape(period, HD)
            values = v_ref[:, k].reshape(period, HD)
            scores = lax.dot_general(query, keys, (((1,), (1,)), ((), ())), preferred_element_type=jnp.float32)
            allowed = lane >= begin - at * period
            if at >= base:
                allowed = allowed & (lane <= q_index - at * period)
            weights = jnp.where(allowed, jnp.exp(scores), 0.0)
            den = den + jnp.sum(weights, axis=1, keepdims=True)
            num = num + jnp.dot(weights.astype(jnp.bfloat16), values, preferred_element_type=jnp.float32)
            at += 1
    context = (num / den).astype(jnp.bfloat16)
    term = jnp.dot(context, w_ref[...], preferred_element_type=jnp.float32)

    @pl.when(head == 0)
    def _():
        total[...] = term

    @pl.when(head > 0)
    def _():
        total[...] += term

    @pl.when(head == pl.num_programs(0) - 1)
    def _():
        width = o_ref.shape[2]
        for z in range(o_ref.shape[0]):
            o_ref[z] = total[:, z * width : (z + 1) * width].astype(jnp.bfloat16)


def attend(meta, queries, kvs, out_weight, shards, docs, stripes):
    rows, head_width = queries.shape
    plane = kvs[0].shape[0]
    size = rows // stripes
    heads = head_width // HD
    operands, specs = [], []
    for kv in kvs:
        kv = kv.reshape(plane, 2, stripes, size, head_width)
        for which in range(2):
            operands.append(kv)
            specs.append(
                pl.BlockSpec((plane, None, stripes, size, HD), lambda h, m, which=which: (0, which, 0, 0, h))
            )
    width = out_weight.shape[1]
    operands.append(out_weight)
    specs.append(pl.BlockSpec((HD, width), lambda h, m: (h, 0)))
    pairs = rows * plane * rows * len(kvs)
    return pl.pallas_call(
        functools.partial(attend_kernel, docs, (len(kvs) - 1) * stripes),
        grid_spec=pltpu.PrefetchScalarGridSpec(
            num_scalar_prefetch=1,
            grid=(heads,),
            in_specs=[pl.BlockSpec((rows, HD), lambda h, m: (0, h))] + specs,
            out_specs=pl.BlockSpec((shards, rows, width // shards), lambda h, m: (0, 0, 0)),
            scratch_shapes=[pltpu.VMEM((rows, width), jnp.float32)],
        ),
        out_shape=jax.ShapeDtypeStruct((shards, rows, width // shards), jnp.bfloat16),
        compiler_params=pltpu.CompilerParams(vmem_limit_bytes=VMEM_LIMIT),
        cost_estimate=pl.CostEstimate(
            flops=4 * pairs * head_width, bytes_accessed=4 * kvs[0].size, transcendentals=pairs * heads
        ),
        name="attend",
    )(meta, queries, *operands)


ORDER = (
    ("first", 0),
    ("first", 1),
    ("hop", 0, 1),
    ("hop", 0, 2),
    ("hop", 0, 3),
    ("pkv", 0),
    ("hop", 1, 1),
    ("own", 0),
    ("pq", 0),
    ("first", 2),
    ("near", 0, 0),
    ("hop", 1, 2),
    ("near", 0, 1),
    ("hop", 1, 3),
    ("hop", 2, 1),
    ("pkv", 1),
    ("first", 3),
    ("far", 0, 0),
    ("own", 1),
    ("hop", 2, 2),
    ("far", 0, 1),
    ("pq", 1),
    ("near", 1, 0),
    ("all", 0),
    ("late", 0),
    ("hop", 3, 1),
    ("out", 0),
    ("near", 1, 1),
    ("rfirst", 0),
    ("hop", 2, 3),
    ("pkv", 2),
    ("own", 2),
    ("pq", 2),
    ("far", 1, 0),
    ("early", 2, 0),
    ("early", 1, 0),
    ("far", 1, 1),
    ("all", 1),
    ("hop", 3, 2),
    ("near", 2, 0),
    ("late", 1),
    ("hop", 3, 3),
    ("out", 1),
    ("rfirst", 1),
    ("round", 0, 1),
    ("pkv", 3),
    ("near", 2, 1),
    ("pq", 3),
    ("own", 3),
    ("far", 2, 0),
    ("early", 2, 1),
    ("round", 0, 2),
    ("far", 2, 1),
    ("early", 3, 0),
    ("all", 2),
    ("late", 2),
    ("round", 1, 1),
    ("out", 2),
    ("round", 1, 2),
    ("rfirst", 2),
    ("near", 3, 0),
    ("near", 3, 1),
    ("final", 0),
    ("round", 2, 1),
    ("early", 3, 1),
    ("far", 3, 0),
    ("far", 3, 1),
    ("early", 3, 2),
    ("round", 2, 2),
    ("all", 3),
    ("final", 1),
    ("late", 3),
    ("out", 3),
    ("rfirst", 3),
    ("round", 3, 1),
    ("round", 3, 2),
    ("final", 2),
    ("final", 3),
)


def line_copy(src, dst, send_sem, recv_sem, to):
    return pltpu.make_async_remote_copy(
        src_ref=src,
        dst_ref=dst,
        send_sem=send_sem,
        recv_sem=recv_sem,
        device_id=to,
        device_id_type=pl.DeviceIdType.MESH,
    )


def block_kernel(
    docs, first_meta, meta_ref, deal_ref, w_hbm, wo_hbm, landed_ref,
    received, x_ref, o_ref, returned, w, wo, xg, normed, query, kv, num, den, context, terms, from_right, from_left, final,
    w_sem, a_send, a_recv, g_send, g_recv, r_send, r_recv, d_send, d_recv, b_send, b_recv,
):
    shards, rows, width = xg.shape
    stripes, plane, _, size, head_width = kv.shape
    heads = head_width // HD
    period = plane * size
    last = shards - 1
    row = lax.broadcasted_iota(jnp.int32, (size, 1), 0)
    x, place, z = lax.axis_index("dp"), lax.axis_index("ctx"), lax.axis_index("tensor")
    y, core = place // 2, lax.rem(place, 2)

    def block(flip_x, flip_y, flip_core):
        return (x ^ flip_x) * 4 + (y ^ flip_y) * 2 + (core ^ flip_core)

    def device(flip_x, flip_y, flip_core):
        return {"dp": x ^ flip_x, "ctx": (y ^ flip_y) * 2 + (core ^ flip_core)}

    def peer(flip):
        flips = flip // 4, (flip // 2) % 2, flip % 2
        return block(*flips), device(*flips)

    me = block(0, 0, 0)
    sibling, across_x, across_y = device(0, 0, 1), device(1, 0, 0), device(0, 1, 0)
    left, right = {"tensor": z - 1}, {"tensor": z + 1}

    loads = [pltpu.make_async_copy(w_hbm.at[p], w.at[p], w_sem.at[p]) for p in range(3)]
    loads.append(pltpu.make_async_copy(wo_hbm, wo, w_sem.at[3]))
    for which in (1, 2, 0, 3):
        loads[which].start()

    barrier = pltpu.get_barrier_semaphore()
    for flip in range(1, plane):
        pl.semaphore_signal(barrier, inc=1, device_id=peer(flip)[1], device_id_type=pl.DeviceIdType.MESH)

    @pl.when(z > 0)
    def _():
        pl.semaphore_signal(barrier, inc=1, device_id=left, device_id_type=pl.DeviceIdType.MESH)

    @pl.when(z < last)
    def _():
        pl.semaphore_signal(barrier, inc=1, device_id=right, device_id_type=pl.DeviceIdType.MESH)

    pl.semaphore_wait(barrier, plane - 1 + jnp.where(z > 0, 1, 0) + jnp.where(z < last, 1, 0))

    def rows_of(s):
        return pl.ds(s * size, size)

    def deal_copy(flip):
        other, target = peer(flip)
        return line_copy(deal_ref.at[other], received.at[me], d_send.at[flip], d_recv.at[flip], target)

    def back_copy(flip):
        other, target = peer(flip)
        return line_copy(returned.at[other], landed_ref.at[me], b_send.at[flip], b_recv.at[flip], target)

    far_first = (6, 7, 4, 5, 2, 3, 1)

    def owned(b, s):
        index = s * period + me * size + row
        return (index >= meta_ref[first_meta + b, 0]) & (index < meta_ref[first_meta + b + 1, 0])

    def deal():
        for flip in far_first:
            deal_copy(flip).start()
        received[me] = deal_ref[me]
        for flip in far_first:
            other, target = peer(flip)
            line_copy(deal_ref.at[other], received.at[other], d_send.at[flip], d_recv.at[flip], target).wait_recv()
        for s in range(stripes):
            picked = jnp.zeros((size, width), jnp.float32)
            for b in range(plane):
                picked = jnp.where(owned(b, s), received[b].astype(jnp.float32), picked)
            x_ref[rows_of(s)] = picked.astype(jnp.bfloat16)

    def give_back():
        for b in range(plane):
            picked = jnp.zeros((size, width), jnp.float32)
            for s in range(stripes):
                picked = jnp.where(owned(b, s), o_ref[rows_of(s)].astype(jnp.float32), picked)
            returned[b] = picked.astype(jnp.bfloat16)
        for flip in far_first:
            back_copy(flip).start()
        landed_ref[me] = returned[me]
        for flip in far_first:
            other, target = peer(flip)
            line_copy(returned.at[other], landed_ref.at[other], b_send.at[flip], b_recv.at[flip], target).wait_recv()
        for flip in far_first:
            deal_copy(flip).wait_send()
            back_copy(flip).wait_send()

    def feature_copy(s, way, hop):
        origin = z + hop if way == 0 else z - hop
        piece = xg.at[origin, rows_of(s)]
        source = x_ref.at[rows_of(s)] if hop == 0 else piece
        return line_copy(source, piece, a_send.at[way, s, hop], a_recv.at[way, s, hop], left if way == 0 else right)

    def feature_sent(way, hop):
        return (z > 0) & (z + hop <= last) if way == 0 else (z < last) & (z - hop >= 0)

    def feature_first(s):
        for way in range(2):

            @pl.when(feature_sent(way, 0))
            def _():
                feature_copy(s, way, 0).start()

    def feature_hop(s, hop):
        for way in range(2):

            @pl.when((z + hop <= last) if way == 0 else (z - hop >= 0))
            def _():
                origin = z + hop if way == 0 else z - hop
                piece = xg.at[origin, rows_of(s)]
                line_copy(
                    piece, piece, a_send.at[way, s, hop - 1], a_recv.at[way, s, hop - 1], left if way == 0 else right
                ).wait_recv()

            if hop < last:

                @pl.when(feature_sent(way, hop))
                def _():
                    feature_copy(s, way, hop).start()

    def feature_end():
        for s in range(stripes):
            for way in range(2):
                for hop in range(last):

                    @pl.when(feature_sent(way, hop))
                    def _():
                        feature_copy(s, way, hop).wait_send()

    first = core == 0
    onward = jnp.where(first, block(0, 1, 0), block(1, 0, 0))
    other = jnp.where(first, block(1, 0, 0), block(0, 1, 0))
    onward_device = {
        "dp": jnp.where(first, x ^ 1, x),
        "ctx": jnp.where(first, place, (y ^ 1) * 2 + core),
    }
    sent = []

    def kv_send(s, half, origin, route, target):
        piece = kv.at[s, origin, half]
        copy = line_copy(piece, piece, g_send.at[s, half, route], g_recv.at[s, half, route], target)
        copy.start()
        sent.append(copy)

    def kv_arrive(s, half, origin, route):
        piece = kv.at[s, origin, half]
        line_copy(piece, piece, g_send.at[s, half, route], g_recv.at[s, half, route], sibling).wait_recv()

    def kv_own(s):
        for half in range(2):
            kv_send(s, half, me, 1, across_x)
            kv_send(s, half, me, 2, across_y)
        for half in range(2):
            kv_send(s, half, me, 0, sibling)

    def kv_near(s, half):
        kv_arrive(s, half, onward, jnp.where(first, 2, 1))
        kv_send(s, half, onward, 3, onward_device)
        kv_send(s, half, onward, jnp.where(first, 5, 4), sibling)
        kv_arrive(s, half, other, jnp.where(first, 1, 2))
        kv_send(s, half, other, jnp.where(first, 4, 5), sibling)

    def kv_far(s, half):
        kv_arrive(s, half, block(1, 1, 0), 3)
        kv_send(s, half, block(1, 1, 0), 6, sibling)

    def kv_all(s):
        for half in range(2):
            kv_arrive(s, half, block(0, 0, 1), 0)
            kv_arrive(s, half, block(1, 0, 1), 4)
            kv_arrive(s, half, block(0, 1, 1), 5)
            kv_arrive(s, half, block(1, 1, 1), 6)

    def normalize(s):
        total = jnp.zeros((size, 1), jnp.float32)
        for j in range(shards):
            wide = xg[j, rows_of(s)].astype(jnp.float32)
            total = total + jnp.sum(wide * wide, axis=1, keepdims=True)
        factor = lax.rsqrt(total / (shards * width) + norm_epsilon)
        for j in range(shards):
            normed[:, j * width : (j + 1) * width] = (xg[j, rows_of(s)].astype(jnp.float32) * factor).astype(
                jnp.bfloat16
            )

    def head_normed(acc, scale):
        parts = []
        for h in range(heads):
            head = acc[:, h * HD : (h + 1) * HD]
            factor = lax.rsqrt(jnp.mean(head * head, axis=1, keepdims=True) + head_epsilon) * scale
            parts.append((head * factor).astype(jnp.bfloat16))
        return parts

    def part_of(which):
        return jnp.dot(normed[...], w[which], preferred_element_type=jnp.float32)

    def project_kv(s):
        normalize(s)
        if s == 0:
            loads[1].wait()
        for h, value in enumerate(head_normed(part_of(1), 1.0)):
            kv[s, me, 0, :, h * HD : (h + 1) * HD] = value
        if s == 0:
            loads[2].wait()
        kv[s, me, 1] = part_of(2).astype(jnp.bfloat16)

    def project_q(s):
        if s == 0:
            loads[0].wait()
        for h, value in enumerate(head_normed(part_of(0), score_scale)):
            query[rows_of(s), h * HD : (h + 1) * HD] = value

    lane = lax.broadcasted_iota(jnp.int32, (1, period), 1)

    def begin_of(s):
        q_index = s * period + me * size + row
        begin = jnp.zeros((size, 1), jnp.int32)
        for d in range(docs):
            at = first_meta + d * (plane // docs)
            begin = jnp.where(q_index >= meta_ref[at, 0], meta_ref[at, 0], begin)
        return begin

    def attend(s, steps):
        begin = begin_of(s)

        def one_head(h, carry):
            at = pl.ds(pl.multiple_of(h * HD, HD), HD)
            lines = query[rows_of(s), at]
            top = jnp.zeros((size, HD), jnp.float32) if steps[0] == 0 else num[s, :, at]
            low = jnp.zeros((size, 1), jnp.float32) if steps[0] == 0 else den[s, :, at][:, :1]
            for t in steps:
                keys = kv[t, :, 0, :, at].reshape(period, HD)
                values = kv[t, :, 1, :, at].reshape(period, HD)
                scores = lax.dot_general(lines, keys, (((1,), (1,)), ((), ())), preferred_element_type=jnp.float32)
                allowed = lane >= begin - t * period
                if t == s:
                    allowed = allowed & (lane <= me * size + row)
                weights = jnp.where(allowed, jnp.exp(scores), 0.0)
                low = low + jnp.sum(weights, axis=1, keepdims=True)
                top = top + jnp.dot(weights.astype(jnp.bfloat16), values, preferred_element_type=jnp.float32)
            if steps[-1] == s:
                context[:, at] = (top / low).astype(jnp.bfloat16)
            else:
                num[s, :, at] = top
                den[s, :, at] = jnp.broadcast_to(low, (size, HD))
            return carry

        lax.fori_loop(0, heads, one_head, 0)

    def early(s, t):
        attend(s, [t])

    def late(s):
        attend(s, [s])

    def project_out(s):
        if s == 0:
            loads[3].wait()
        for j in range(shards):
            terms[s, j] = jnp.dot(
                context[...], wo[:, j * width : (j + 1) * width], preferred_element_type=jnp.float32
            ).astype(jnp.bfloat16)

    def sum_copy(s, way, d):
        land = from_right if way == 0 else from_left
        return line_copy(
            terms.at[s, d], land.at[s, d], r_send.at[way, s, d], r_recv.at[way, s, d], left if way == 0 else right
        )

    def sum_sent(way, d):
        return (z > d) if way == 0 else (z < d)

    def sum_first(s):
        for way in range(2):
            for k in range(last):

                @pl.when(z == (last if way == 0 else 0))
                def _():
                    sum_copy(s, way, k if way == 0 else last - k).start()

    def sum_round(s, r):
        for way in range(2):
            land = from_right if way == 0 else from_left
            k = r - last + z if way == 0 else r - z
            d = k if way == 0 else last - k

            @pl.when((k >= 0) & ((z < last) if way == 0 else (z > 0)))
            def _():
                sum_copy(s, way, d).wait_recv()
                terms[s, d] = (terms[s, d].astype(jnp.float32) + land[s, d].astype(jnp.float32)).astype(jnp.bfloat16)
                sum_copy(s, way, d).start()

    def sum_final(s):
        final[...] = terms[s, z].astype(jnp.float32)
        for way in range(2):
            land = from_right if way == 0 else from_left

            @pl.when((z < last) if way == 0 else (z > 0))
            def _():
                sum_copy(s, way, z).wait_recv()
                final[...] += land[s, z].astype(jnp.float32)

        o_ref[rows_of(s)] = final[...].astype(jnp.bfloat16)

    def sum_end():
        for s in range(stripes):
            for way in range(2):
                for d in range(shards):

                    @pl.when(sum_sent(way, d))
                    def _():
                        sum_copy(s, way, d).wait_send()

    deal()
    for s in range(stripes):
        xg[z, rows_of(s)] = x_ref[rows_of(s)]
    steps = {
        "first": feature_first,
        "hop": feature_hop,
        "pkv": project_kv,
        "pq": project_q,
        "own": kv_own,
        "near": kv_near,
        "far": kv_far,
        "all": kv_all,
        "early": early,
        "late": late,
        "out": project_out,
        "rfirst": sum_first,
        "round": sum_round,
        "final": sum_final,
    }
    for name, *at in ORDER:
        steps[name](*at)
    give_back()
    feature_end()
    for copy in sent:
        copy.wait_send()
    sum_end()


def block(meta, first_meta, dealt, weight, out_weight, docs, shards, stripes, call):
    plane, size, width = dealt.shape
    rows = stripes * size
    head_width = weight.shape[2]
    full = out_weight.shape[1]
    sixteen = jnp.bfloat16
    dma = pltpu.SemaphoreType.DMA
    return pl.pallas_call(
        functools.partial(block_kernel, docs, first_meta),
        in_specs=[
            pl.BlockSpec(memory_space=pltpu.SMEM),
            pl.BlockSpec(memory_space=pltpu.VMEM),
            pl.BlockSpec(memory_space=pl.ANY),
            pl.BlockSpec(memory_space=pl.ANY),
        ],
        out_specs=pl.BlockSpec(memory_space=pltpu.VMEM),
        out_shape=jax.ShapeDtypeStruct((plane, size, width), sixteen),
        scratch_shapes=[
            pltpu.VMEM((plane, size, width), sixteen),
            pltpu.VMEM((rows, width), sixteen),
            pltpu.VMEM((rows, width), sixteen),
            pltpu.VMEM((plane, size, width), sixteen),
            pltpu.VMEM(weight.shape, sixteen),
            pltpu.VMEM(out_weight.shape, sixteen),
            pltpu.VMEM((shards, rows, width), sixteen),
            pltpu.VMEM((size, full), sixteen),
            pltpu.VMEM((rows, head_width), sixteen),
            pltpu.VMEM((stripes, plane, 2, size, head_width), sixteen),
            pltpu.VMEM((stripes, size, head_width), jnp.float32),
            pltpu.VMEM((stripes, size, head_width), jnp.float32),
            pltpu.VMEM((size, head_width), sixteen),
            pltpu.VMEM((stripes, shards, size, width), sixteen),
            pltpu.VMEM((stripes, shards, size, width), sixteen),
            pltpu.VMEM((stripes, shards, size, width), sixteen),
            pltpu.VMEM((size, width), jnp.float32),
            dma((4,)),
            dma((2, stripes, shards)),
            dma((2, stripes, shards)),
            dma((stripes, 2, 7)),
            dma((stripes, 2, 7)),
            dma((2, stripes, shards)),
            dma((2, stripes, shards)),
            dma((plane,)),
            dma((plane,)),
            dma((plane,)),
            dma((plane,)),
        ],
        compiler_params=pltpu.CompilerParams(
            collective_id=call, has_side_effects=True, vmem_limit_bytes=VMEM_LIMIT
        ),
        cost_estimate=pl.CostEstimate(flops=10_000_000_000, bytes_accessed=100_000_000, transcendentals=0),
        name="block",
    )(meta, dealt, weight, out_weight)


LINES = 32


def count_kernel(depth_ref, place_ref, info_ref, mine, landed, send_sem, recv_sem):
    plane = landed.shape[0]
    lines, lanes = depth_ref.shape
    ctx_count = lax.axis_size("ctx")
    x, place = lax.axis_index("dp"), lax.axis_index("ctx")
    me = x * ctx_count + place

    def device(flip):
        return {"dp": x ^ (flip // ctx_count), "ctx": place ^ (flip % ctx_count)}

    barrier = pltpu.get_barrier_semaphore()
    for flip in range(1, plane):
        pl.semaphore_signal(barrier, inc=1, device_id=device(flip), device_id_type=pl.DeviceIdType.MESH)
    active = depth_ref[...] >= RECURSION
    ones = jnp.where(active, 1.0, 0.0)
    total = jnp.sum(jnp.sum(ones, axis=1, keepdims=True), axis=0, keepdims=True)
    mine[...] = jnp.broadcast_to(total, mine.shape).astype(jnp.int32)
    pl.semaphore_wait(barrier, plane - 1)

    def copy(flip, slot):
        return line_copy(mine, landed.at[slot], send_sem.at[flip], recv_sem.at[flip], device(flip))

    for flip in range(1, plane):
        copy(flip, me).start()
    landed[me] = mine[...]
    upto = lax.broadcasted_iota(jnp.int32, (lanes, lanes), 0) <= lax.broadcasted_iota(jnp.int32, (lanes, lanes), 1)
    inside = jnp.dot(
        ones.astype(jnp.bfloat16), jnp.where(upto, 1.0, 0.0).astype(jnp.bfloat16), preferred_element_type=jnp.float32
    )
    ahead = lax.broadcasted_iota(jnp.int32, (lines, lines), 1) < lax.broadcasted_iota(jnp.int32, (lines, lines), 0)
    line_total = jnp.broadcast_to(inside[:, lanes - 1 :], (lines, lanes))
    before = jnp.dot(
        jnp.where(ahead, 1.0, 0.0).astype(jnp.bfloat16),
        line_total.astype(jnp.bfloat16),
        preferred_element_type=jnp.float32,
    )
    for flip in range(1, plane):
        copy(flip, me ^ flip).wait_recv()
    start = jnp.zeros((1, lanes), jnp.int32)
    running = jnp.zeros((1, lanes), jnp.int32)
    for b in range(plane):
        info_ref[lines + b : lines + b + 1] = running
        count = landed[b, 0:1]
        start = start + jnp.where(me > b, count, 0)
        running = running + count
    for b in range(plane, info_ref.shape[0] - lines):
        info_ref[lines + b : lines + b + 1] = running
    base = (start & (CAP - 1)) + before.astype(jnp.int32)
    info_ref[:lines] = base
    place_ref[...] = jnp.where(active, base + inside.astype(jnp.int32) - 1, -1)
    for flip in range(1, plane):
        copy(flip, me).wait_send()


def count(depth, plane, call):
    lines = LINES
    lanes = depth.shape[0] // lines
    whole = jnp.int32
    return pl.pallas_call(
        count_kernel,
        in_specs=[pl.BlockSpec(memory_space=pltpu.VMEM)],
        out_specs=[pl.BlockSpec(memory_space=pltpu.VMEM)] * 2,
        out_shape=[
            jax.ShapeDtypeStruct((lines, lanes), whole),
            jax.ShapeDtypeStruct((lines + 16, lanes), whole),
        ],
        scratch_shapes=[
            pltpu.VMEM((8, lanes), whole),
            pltpu.VMEM((plane, 8, lanes), whole),
            pltpu.SemaphoreType.DMA((plane,)),
            pltpu.SemaphoreType.DMA((plane,)),
        ],
        compiler_params=pltpu.CompilerParams(collective_id=call, has_side_effects=True),
        name="count",
    )(depth.reshape(lines, lanes))


ALIGN = 16
GROUP = 2
LOADS = 8


def onehot_of(place_ref, at, floor, window):
    wanted = jnp.concatenate([place_ref[pl.ds(at + i, 1), :] for i in range(GROUP)], axis=1)
    spot = lax.broadcasted_iota(jnp.int32, (window, wanted.shape[1]), 0)
    return jnp.where(spot + floor == wanted, 1.0, 0.0).astype(jnp.bfloat16)


def compact_kernel(info_ref, place_ref, tokens_hbm, out_ref, tokens, buffer, sems):
    lines, lanes = place_ref.shape
    block_rows = GROUP * lanes
    window = block_rows + ALIGN
    chunk = tokens.shape[0] // LOADS
    loads = []
    for i in range(LOADS):
        rows = pl.ds(i * chunk, chunk)
        loads.append(pltpu.make_async_copy(tokens_hbm.at[rows], tokens.at[rows], sems.at[i]))
        loads[-1].start()
    start = info_ref[0, 0]
    edge = lax.broadcasted_iota(jnp.int32, (ALIGN, 1), 0)
    for i in range(lines // GROUP):
        if (i * block_rows) % chunk == 0:
            loads[i * block_rows // chunk].wait()
        base = info_ref[i * GROUP, 0]
        floor = pl.multiple_of(base - lax.rem(base, ALIGN), ALIGN)
        spread = onehot_of(place_ref, i * GROUP, floor, window)
        rows = tokens[i * block_rows : (i + 1) * block_rows]
        found = jnp.dot(spread, rows, preferred_element_type=jnp.float32)
        old = buffer[pl.ds(floor, ALIGN)].astype(jnp.float32)
        seam = jnp.where(edge < base - floor, old, found[:ALIGN])
        buffer[pl.ds(floor, ALIGN)] = seam.astype(jnp.bfloat16)
        buffer[pl.ds(floor + ALIGN, block_rows)] = found[ALIGN:].astype(jnp.bfloat16)
    plane, size, _ = out_ref.shape
    for b in range(plane):
        spot = b * size + lax.broadcasted_iota(jnp.int32, (size, 1), 0)
        low = buffer[b * size : (b + 1) * size].astype(jnp.float32)
        high = buffer[CAP + b * size : CAP + (b + 1) * size].astype(jnp.float32)
        out_ref[b] = jnp.where(spot >= start, low, high).astype(jnp.bfloat16)


def compact(info, places, tokens, plane):
    lines, lanes = places.shape
    width = tokens.shape[1]
    return pl.pallas_call(
        compact_kernel,
        in_specs=[
            pl.BlockSpec(memory_space=pltpu.SMEM),
            pl.BlockSpec(memory_space=pltpu.VMEM),
            pl.BlockSpec(memory_space=pl.ANY),
        ],
        out_specs=pl.BlockSpec(memory_space=pltpu.VMEM),
        out_shape=jax.ShapeDtypeStruct((plane, CAP // plane, width), tokens.dtype),
        scratch_shapes=[
            pltpu.VMEM(tokens.shape, tokens.dtype),
            pltpu.VMEM((2 * CAP + GROUP * lanes + ALIGN, width), tokens.dtype),
            pltpu.SemaphoreType.DMA((LOADS,)),
        ],
        compiler_params=pltpu.CompilerParams(vmem_limit_bytes=VMEM_LIMIT),
        name="compact",
    )(info, places, tokens)


def unpack_kernel(info_ref, place_ref, landed_ref, out_hbm, buffer, columns, out, sems):
    lines, lanes = place_ref.shape
    window = 2 * lanes
    buffer[:CAP] = landed_ref[...]
    buffer[CAP:] = landed_ref[: buffer.shape[0] - CAP]
    columns[...] = jnp.transpose(place_ref[...])
    spot = lax.broadcasted_iota(jnp.int32, (lanes, window), 1)
    chunk = out.shape[0] // LOADS
    stores = []
    for i in range(lines):
        base = info_ref[i, 0]
        floor = base - lax.rem(base, ALIGN)
        spread = jnp.where(columns[:, i : i + 1] - floor == spot, 1.0, 0.0).astype(jnp.bfloat16)
        rows = buffer[pl.ds(pl.multiple_of(lax.rem(floor, CAP), ALIGN), window)]
        out[i * lanes : (i + 1) * lanes] = jnp.dot(spread, rows, preferred_element_type=jnp.float32).astype(
            jnp.bfloat16
        )
        if (i + 1) * lanes % chunk == 0:
            at = pl.ds((i + 1) * lanes - chunk, chunk)
            stores.append(pltpu.make_async_copy(out.at[at], out_hbm.at[at], sems.at[len(stores)]))
            stores[-1].start()
    for store in stores:
        store.wait()


def unpack(info, places, landed, length):
    lines, lanes = places.shape
    width = landed.shape[1]
    return pl.pallas_call(
        unpack_kernel,
        in_specs=[
            pl.BlockSpec(memory_space=pltpu.SMEM),
            pl.BlockSpec(memory_space=pltpu.VMEM),
            pl.BlockSpec(memory_space=pltpu.VMEM),
        ],
        out_specs=pl.BlockSpec(memory_space=pl.ANY),
        out_shape=jax.ShapeDtypeStruct((length, width), landed.dtype),
        scratch_shapes=[
            pltpu.VMEM((CAP + 2 * lanes, width), landed.dtype),
            pltpu.VMEM((lanes, lines), jnp.int32),
            pltpu.VMEM((length, width), landed.dtype),
            pltpu.SemaphoreType.DMA((LOADS,)),
        ],
        compiler_params=pltpu.CompilerParams(vmem_limit_bytes=VMEM_LIMIT),
        name="unpack",
    )(info, places, landed)


def per_device(hidden, depth, qkv_weight, out_weight):
    tokens = hidden[0]
    local_len = tokens.shape[0]
    docs = lax.axis_size("dp")
    ctx_count = lax.axis_size("ctx")
    shards = lax.axis_size("tensor")
    plane = docs * ctx_count
    me = lax.axis_index("dp") * ctx_count + lax.axis_index("ctx")
    size = CAP // plane
    stripes = ACT_DEV // size

    if (docs, ctx_count) == (2, 4) and local_len % (LINES * 128) == 0 and stripes >= 2 and shards >= 2:
        places, info = count(depth[0], plane, 0)
        dealt = compact(info, places, tokens, plane)
        weight = jnp.transpose(qkv_weight, (1, 0, 2))
        landed = block(info, LINES, dealt, weight, out_weight, docs, shards, stripes, 1)
        return unpack(info, places, landed.reshape(CAP, -1), local_len)[None]

    active = depth[0] >= RECURSION
    ones = active.astype(jnp.int32)
    counts = lax.all_gather(jnp.sum(ones)[None], PLANE, axis=0, tiled=True)
    ends = jnp.cumsum(counts)
    starts = ends - counts
    rank = jnp.cumsum(ones) - 1
    slot = jnp.where(active, lax.rem(starts[me] + rank, CAP), -1)
    onehot = (jnp.arange(CAP, dtype=jnp.int32)[:, None] == slot[None, :]).astype(jnp.bfloat16)
    dealt = jnp.dot(onehot, tokens, preferred_element_type=jnp.float32).astype(jnp.bfloat16)
    received = lax.all_to_all(dealt.reshape(plane, size, -1), PLANE, 0, 0)

    index = (
        jnp.arange(stripes, dtype=jnp.int32)[:, None] * CAP
        + me * size
        + jnp.arange(size, dtype=jnp.int32)[None, :]
    )
    owned = (index[None] >= starts[:, None, None]) & (index[None] < ends[:, None, None])
    zero = jnp.zeros((), jnp.bfloat16)
    packed = jnp.where(owned[0][:, :, None], received[0][None], zero)
    for b in range(1, plane):
        packed = jnp.where(owned[b][:, :, None], received[b][None], packed)
    packed = packed.reshape(ACT_DEV, -1)

    chunks = 2
    chunk_stripes = stripes // chunks
    chunk_rows = ACT_DEV // chunks
    weight = jnp.transpose(qkv_weight, (1, 0, 2))
    meta = jnp.concatenate([starts[::ctx_count], me[None]]).astype(jnp.int32)
    rows_all = [
        lax.all_gather(packed[c * chunk_rows : (c + 1) * chunk_rows], "tensor", axis=0) for c in range(chunks)
    ]
    kvs, backs = [], []
    for c in range(chunks):
        queries, kv = project(rows_all[c], weight)
        kvs.append(lax.all_gather(kv, PLANE, axis=0))
        terms = attend(meta, queries, kvs, out_weight, shards, docs, chunk_stripes)
        backs.append(lax.psum_scatter(terms, "tensor", scatter_dimension=0))
    rows_back = jnp.concatenate(backs, axis=0)

    rows_back = rows_back.reshape(stripes, size, -1)
    returned = jnp.where(owned[:, 0][:, :, None], rows_back[0][None], zero)
    for k in range(1, stripes):
        returned = jnp.where(owned[:, k][:, :, None], rows_back[k][None], returned)
    landed = lax.all_to_all(returned, PLANE, 0, 0).reshape(CAP, -1)
    spread = (slot[:, None] == jnp.arange(CAP, dtype=jnp.int32)[None, :]).astype(jnp.bfloat16)
    update = jnp.dot(spread, landed, preferred_element_type=jnp.float32).astype(jnp.bfloat16)
    return update[None]


def solution(mesh):
    placed = (P("dp", "ctx", "tensor"), P("dp", "ctx"), P(None, None, "tensor"), P("tensor", None))
    return jax.shard_map(
        per_device, mesh=mesh, in_specs=placed, out_specs=P("dp", "ctx", "tensor"), check_vma=False
    )
```

```python
import functools

import jax
import jax.numpy as jnp
from jax import lax
from jax.experimental import pallas as pl
from jax.experimental.pallas import tpu as pltpu
from jax.sharding import PartitionSpec as P

HD = 128
RECURSION = 3
CAP = 1024
ACT_DEV = 512

score_scale = 0.25
norm_epsilon = 1e-05
head_epsilon = 1e-06
VMEM_LIMIT = 60 * 1024 * 1024
PLANE = ("dp", "ctx")


def project_kernel(x_ref, w_ref, q_ref, kv_ref, normed):
    part = pl.program_id(0)
    shards, rows, width = x_ref.shape

    @pl.when(part == 0)
    def _():
        total = jnp.zeros((rows, 1), jnp.float32)
        for z in range(shards):
            wide = x_ref[z].astype(jnp.float32)
            total = total + jnp.sum(wide * wide, axis=1, keepdims=True)
        factor = lax.rsqrt(total / (shards * width) + norm_epsilon)
        for z in range(shards):
            normed[z] = (x_ref[z].astype(jnp.float32) * factor).astype(jnp.bfloat16)

    acc = jnp.dot(normed[0], w_ref[0, :width], preferred_element_type=jnp.float32)
    for z in range(1, shards):
        acc = acc + jnp.dot(normed[z], w_ref[0, z * width : (z + 1) * width], preferred_element_type=jnp.float32)
    heads = acc.shape[1] // HD

    def head_normed(scale):
        parts = []
        for h in range(heads):
            head = acc[:, h * HD : (h + 1) * HD]
            factor = lax.rsqrt(jnp.mean(head * head, axis=1, keepdims=True) + head_epsilon) * scale
            parts.append((head * factor).astype(jnp.bfloat16))
        return parts

    @pl.when(part == 0)
    def _():
        for h, value in enumerate(head_normed(score_scale)):
            q_ref[:, h * HD : (h + 1) * HD] = value

    @pl.when(part == 1)
    def _():
        for h, value in enumerate(head_normed(1.0)):
            kv_ref[0, :, h * HD : (h + 1) * HD] = value

    @pl.when(part == 2)
    def _():
        kv_ref[0] = acc.astype(jnp.bfloat16)


def project(rows_all, weight):
    shards, rows, width = rows_all.shape
    head_width = weight.shape[2]
    flops = 2 * rows * shards * width * 3 * head_width
    return pl.pallas_call(
        project_kernel,
        grid=(3,),
        out_shape=[
            jax.ShapeDtypeStruct((rows, head_width), jnp.bfloat16),
            jax.ShapeDtypeStruct((2, rows, head_width), jnp.bfloat16),
        ],
        in_specs=[
            pl.BlockSpec((shards, rows, width), lambda p: (0, 0, 0)),
            pl.BlockSpec((1, shards * width, head_width), lambda p: (p, 0, 0)),
        ],
        out_specs=[
            pl.BlockSpec((rows, head_width), lambda p: (0, 0)),
            pl.BlockSpec((1, rows, head_width), lambda p: (jnp.maximum(p - 1, 0), 0, 0)),
        ],
        scratch_shapes=[pltpu.VMEM((shards, rows, width), jnp.bfloat16)],
        compiler_params=pltpu.CompilerParams(vmem_limit_bytes=VMEM_LIMIT),
        cost_estimate=pl.CostEstimate(flops=flops, bytes_accessed=2 * weight.size, transcendentals=0),
        name="project",
    )(rows_all, weight)


def attend_kernel(docs, base, meta_ref, q_ref, *refs):
    w_ref, o_ref, total = refs[-3:]
    pairs = [(refs[i], refs[i + 1]) for i in range(0, len(refs) - 3, 2)]
    head = pl.program_id(0)
    plane, stripes, size, _ = refs[0].shape
    period = plane * size
    rows = stripes * size
    me = meta_ref[docs]
    row = lax.broadcasted_iota(jnp.int32, (rows, 1), 0)
    q_index = (base + row // size) * period + me * size + lax.rem(row, size)
    begin = jnp.zeros((rows, 1), jnp.int32)
    for d in range(docs):
        begin = jnp.where(q_index >= meta_ref[d], meta_ref[d], begin)
    lane = lax.broadcasted_iota(jnp.int32, (1, period), 1)
    query = q_ref[...]
    num = jnp.zeros((rows, HD), jnp.float32)
    den = jnp.zeros((rows, 1), jnp.float32)
    at = 0
    for k_ref, v_ref in pairs:
        for k in range(stripes):
            keys = k_ref[:, k].reshape(period, HD)
            values = v_ref[:, k].reshape(period, HD)
            scores = lax.dot_general(query, keys, (((1,), (1,)), ((), ())), preferred_element_type=jnp.float32)
            allowed = lane >= begin - at * period
            if at >= base:
                allowed = allowed & (lane <= q_index - at * period)
            weights = jnp.where(allowed, jnp.exp(scores), 0.0)
            den = den + jnp.sum(weights, axis=1, keepdims=True)
            num = num + jnp.dot(weights.astype(jnp.bfloat16), values, preferred_element_type=jnp.float32)
            at += 1
    context = (num / den).astype(jnp.bfloat16)
    term = jnp.dot(context, w_ref[...], preferred_element_type=jnp.float32)

    @pl.when(head == 0)
    def _():
        total[...] = term

    @pl.when(head > 0)
    def _():
        total[...] += term

    @pl.when(head == pl.num_programs(0) - 1)
    def _():
        width = o_ref.shape[2]
        for z in range(o_ref.shape[0]):
            o_ref[z] = total[:, z * width : (z + 1) * width].astype(jnp.bfloat16)


def attend(meta, queries, kvs, out_weight, shards, docs, stripes):
    rows, head_width = queries.shape
    plane = kvs[0].shape[0]
    size = rows // stripes
    heads = head_width // HD
    operands, specs = [], []
    for kv in kvs:
        kv = kv.reshape(plane, 2, stripes, size, head_width)
        for which in range(2):
            operands.append(kv)
            specs.append(
                pl.BlockSpec((plane, None, stripes, size, HD), lambda h, m, which=which: (0, which, 0, 0, h))
            )
    width = out_weight.shape[1]
    operands.append(out_weight)
    specs.append(pl.BlockSpec((HD, width), lambda h, m: (h, 0)))
    pairs = rows * plane * rows * len(kvs)
    return pl.pallas_call(
        functools.partial(attend_kernel, docs, (len(kvs) - 1) * stripes),
        grid_spec=pltpu.PrefetchScalarGridSpec(
            num_scalar_prefetch=1,
            grid=(heads,),
            in_specs=[pl.BlockSpec((rows, HD), lambda h, m: (0, h))] + specs,
            out_specs=pl.BlockSpec((shards, rows, width // shards), lambda h, m: (0, 0, 0)),
            scratch_shapes=[pltpu.VMEM((rows, width), jnp.float32)],
        ),
        out_shape=jax.ShapeDtypeStruct((shards, rows, width // shards), jnp.bfloat16),
        compiler_params=pltpu.CompilerParams(vmem_limit_bytes=VMEM_LIMIT),
        cost_estimate=pl.CostEstimate(
            flops=4 * pairs * head_width, bytes_accessed=4 * kvs[0].size, transcendentals=pairs * heads
        ),
        name="attend",
    )(meta, queries, *operands)


ORDER = (
    ("dsend", 0),
    ("dsend", 1),
    ("dwait", 0),
    ("dsel", 0, 0),
    ("dsel", 3, 0),
    ("first", 0, 0),
    ("hop", 0, 0, 1),
    ("dwait", 1),
    ("dsel", 0, 1),
    ("dsel", 1, 0),
    ("first", 0, 1),
    ("hop", 0, 0, 2),
    ("hop", 0, 0, 3),
    ("dsel", 2, 1),
    ("hop", 0, 1, 1),
    ("dsel", 1, 1),
    ("first", 1, 1),
    ("hop", 0, 1, 2),
    ("hop", 0, 1, 3),
    ("first", 2, 1),
    ("dsel", 2, 0),
    ("hop", 1, 1, 1),
    ("pkv", 0),
    ("first", 3, 0),
    ("own", 0),
    ("first", 1, 0),
    ("near", 0, 0),
    ("hop", 1, 1, 2),
    ("first", 2, 0),
    ("dsel", 3, 1),
    ("hop", 1, 0, 1),
    ("hop", 1, 1, 3),
    ("near", 0, 1),
    ("pq", 0),
    ("hop", 1, 0, 2),
    ("hop", 1, 0, 3),
    ("first", 3, 1),
    ("pkv", 1),
    ("hop", 2, 0, 1),
    ("far", 0, 0),
    ("hop", 2, 1, 1),
    ("far", 0, 1),
    ("own", 1),
    ("pq", 1),
    ("all", 0),
    ("late", 0),
    ("out", 0),
    ("hop", 2, 1, 2),
    ("hop", 2, 0, 2),
    ("hop", 3, 1, 1),
    ("rfirst", 0, 1),
    ("near", 1, 0),
    ("near", 1, 1),
    ("hop", 2, 1, 3),
    ("hop", 3, 0, 1),
    ("hop", 2, 0, 3),
    ("pkv", 2),
    ("pq", 2),
    ("rfirst", 0, 0),
    ("own", 2),
    ("far", 1, 0),
    ("round", 0, 1, 1),
    ("early", 2, 0),
    ("far", 1, 1),
    ("early", 1, 0),
    ("hop", 3, 1, 2),
    ("all", 1),
    ("late", 1),
    ("hop", 3, 1, 3),
    ("near", 2, 0),
    ("out", 1),
    ("rfirst", 1, 0),
    ("hop", 3, 0, 2),
    ("round", 0, 0, 1),
    ("hop", 3, 0, 3),
    ("pkv", 3),
    ("near", 2, 1),
    ("early", 2, 1),
    ("rfirst", 1, 1),
    ("own", 3),
    ("far", 2, 0),
    ("far", 2, 1),
    ("all", 2),
    ("late", 2),
    ("round", 0, 1, 2),
    ("out", 2),
    ("near", 3, 0),
    ("round", 0, 0, 2),
    ("round", 1, 1, 1),
    ("rfirst", 2, 0),
    ("pq", 3),
    ("rfirst", 2, 1),
    ("round", 1, 0, 1),
    ("early", 3, 0),
    ("near", 3, 1),
    ("early", 3, 1),
    ("round", 2, 0, 1),
    ("round", 1, 0, 2),
    ("round", 1, 1, 2),
    ("far", 3, 0),
    ("early", 3, 2),
    ("far", 3, 1),
    ("round", 2, 0, 2),
    ("all", 3),
    ("round", 2, 1, 1),
    ("final", 1, 0),
    ("late", 3),
    ("out", 3),
    ("rfirst", 3, 0),
    ("final", 1, 1),
    ("final", 0, 1),
    ("rfirst", 3, 1),
    ("final", 2, 0),
    ("final", 0, 0),
    ("round", 3, 0, 1),
    ("round", 3, 0, 2),
    ("round", 3, 1, 1),
    ("round", 2, 1, 2),
    ("final", 3, 0),
    ("bsend", 0),
    ("round", 3, 1, 2),
    ("final", 2, 1),
    ("final", 3, 1),
    ("bsend", 1),
    ("bwait", 0),
    ("bwait", 1),
)


def line_copy(src, dst, send_sem, recv_sem, to):
    return pltpu.make_async_remote_copy(
        src_ref=src,
        dst_ref=dst,
        send_sem=send_sem,
        recv_sem=recv_sem,
        device_id=to,
        device_id_type=pl.DeviceIdType.MESH,
    )


def block_kernel(
    docs, first_meta, meta_ref, deal_ref, w_hbm, wo_hbm, landed_ref,
    received, x_ref, o_ref, returned, w, wo, xg, normed, query, kv, num, den, context, terms, from_right, from_left, final,
    w_sem, a_send, a_recv, g_send, g_recv, r_send, r_recv, d_send, d_recv, b_send, b_recv,
):
    shards, rows, width = xg.shape
    stripes, plane, _, size, head_width = kv.shape
    heads = head_width // HD
    period = plane * size
    last = shards - 1
    row = lax.broadcasted_iota(jnp.int32, (size, 1), 0)
    x, place, z = lax.axis_index("dp"), lax.axis_index("ctx"), lax.axis_index("tensor")
    y, core = place // 2, lax.rem(place, 2)

    def block(flip_x, flip_y, flip_core):
        return (x ^ flip_x) * 4 + (y ^ flip_y) * 2 + (core ^ flip_core)

    def device(flip_x, flip_y, flip_core):
        return {"dp": x ^ flip_x, "ctx": (y ^ flip_y) * 2 + (core ^ flip_core)}

    def peer(flip):
        flips = flip // 4, (flip // 2) % 2, flip % 2
        return block(*flips), device(*flips)

    me = block(0, 0, 0)
    sibling, across_x, across_y = device(0, 0, 1), device(1, 0, 0), device(0, 1, 0)
    left, right = {"tensor": z - 1}, {"tensor": z + 1}

    loads = [pltpu.make_async_copy(w_hbm.at[p], w.at[p], w_sem.at[p]) for p in range(3)]
    loads.append(pltpu.make_async_copy(wo_hbm, wo, w_sem.at[3]))
    for which in (1, 2, 0, 3):
        loads[which].start()

    barrier = pltpu.get_barrier_semaphore()
    for flip in range(1, plane):
        pl.semaphore_signal(barrier, inc=1, device_id=peer(flip)[1], device_id_type=pl.DeviceIdType.MESH)

    @pl.when(z > 0)
    def _():
        pl.semaphore_signal(barrier, inc=1, device_id=left, device_id_type=pl.DeviceIdType.MESH)

    @pl.when(z < last)
    def _():
        pl.semaphore_signal(barrier, inc=1, device_id=right, device_id_type=pl.DeviceIdType.MESH)

    pl.semaphore_wait(barrier, plane - 1 + jnp.where(z > 0, 1, 0) + jnp.where(z < last, 1, 0))

    def rows_of(s):
        return pl.ds(s * size, size)

    half = size // 2

    def part_of_rows(s, part):
        return pl.ds(s * size + part * half, half)

    def part_rows(part):
        return pl.ds(part * half, half)

    def deal_copy(part, flip, origin):
        other, target = peer(flip)
        at = part_rows(part)
        return line_copy(
            deal_ref.at[other, at], received.at[origin, at], d_send.at[part, flip], d_recv.at[part, flip], target
        )

    def back_copy(part, flip, origin):
        other, target = peer(flip)
        at = part_rows(part)
        return line_copy(
            returned.at[other, at], landed_ref.at[origin, at], b_send.at[part, flip], b_recv.at[part, flip], target
        )

    far_first = (6, 7, 4, 5, 2, 3, 1)

    def owned(b, s, part):
        index = s * period + me * size + part * half + row[:half]
        return (index >= meta_ref[first_meta + b, 0]) & (index < meta_ref[first_meta + b + 1, 0])

    def deal_send(part):
        for flip in far_first:
            deal_copy(part, flip, me).start()
        received[me, part_rows(part)] = deal_ref[me, part_rows(part)]

    def deal_wait(part):
        for flip in far_first:
            deal_copy(part, flip, peer(flip)[0]).wait_recv()

    def deal_pick(s, part):
        picked = jnp.zeros((half, width), jnp.float32)
        for b in range(plane):
            picked = jnp.where(owned(b, s, part), received[b, part_rows(part)].astype(jnp.float32), picked)
        picked = picked.astype(jnp.bfloat16)
        x_ref[part_of_rows(s, part)] = picked
        xg[z, part_of_rows(s, part)] = picked

    def back_send(part):
        for b in range(plane):
            picked = jnp.zeros((half, width), jnp.float32)
            for s in range(stripes):
                picked = jnp.where(owned(b, s, part), o_ref[part_of_rows(s, part)].astype(jnp.float32), picked)
            returned[b, part_rows(part)] = picked.astype(jnp.bfloat16)
        for flip in far_first:
            back_copy(part, flip, me).start()
        landed_ref[me, part_rows(part)] = returned[me, part_rows(part)]

    def back_wait(part):
        for flip in far_first:
            back_copy(part, flip, peer(flip)[0]).wait_recv()

    def deal_end():
        for part in range(2):
            for flip in far_first:
                deal_copy(part, flip, me).wait_send()
                back_copy(part, flip, me).wait_send()

    def feature_copy(s, part, way, hop):
        origin = z + hop if way == 0 else z - hop
        at = part_of_rows(s, part)
        piece = xg.at[origin, at]
        source = x_ref.at[at] if hop == 0 else piece
        return line_copy(
            source, piece, a_send.at[way, s, part, hop], a_recv.at[way, s, part, hop], left if way == 0 else right
        )

    def feature_sent(way, hop):
        return (z > 0) & (z + hop <= last) if way == 0 else (z < last) & (z - hop >= 0)

    def feature_first(s, part):
        for way in range(2):

            @pl.when(feature_sent(way, 0))
            def _():
                feature_copy(s, part, way, 0).start()

    def feature_hop(s, part, hop):
        for way in range(2):

            @pl.when((z + hop <= last) if way == 0 else (z - hop >= 0))
            def _():
                origin = z + hop if way == 0 else z - hop
                piece = xg.at[origin, part_of_rows(s, part)]
                line_copy(
                    piece,
                    piece,
                    a_send.at[way, s, part, hop - 1],
                    a_recv.at[way, s, part, hop - 1],
                    left if way == 0 else right,
                ).wait_recv()

            if hop < last:

                @pl.when(feature_sent(way, hop))
                def _():
                    feature_copy(s, part, way, hop).start()

    def feature_end():
        for s in range(stripes):
            for part in range(2):
                for way in range(2):
                    for hop in range(last):

                        @pl.when(feature_sent(way, hop))
                        def _():
                            feature_copy(s, part, way, hop).wait_send()

    first = core == 0
    onward = jnp.where(first, block(0, 1, 0), block(1, 0, 0))
    other = jnp.where(first, block(1, 0, 0), block(0, 1, 0))
    onward_device = {
        "dp": jnp.where(first, x ^ 1, x),
        "ctx": jnp.where(first, place, (y ^ 1) * 2 + core),
    }
    sent = []

    def kv_send(s, half, origin, route, target):
        piece = kv.at[s, origin, half]
        copy = line_copy(piece, piece, g_send.at[s, half, route], g_recv.at[s, half, route], target)
        copy.start()
        sent.append(copy)

    def kv_arrive(s, half, origin, route):
        piece = kv.at[s, origin, half]
        line_copy(piece, piece, g_send.at[s, half, route], g_recv.at[s, half, route], sibling).wait_recv()

    def kv_own(s):
        for half in range(2):
            kv_send(s, half, me, 1, across_x)
            kv_send(s, half, me, 2, across_y)
        for half in range(2):
            kv_send(s, half, me, 0, sibling)

    def kv_near(s, half):
        kv_arrive(s, half, onward, jnp.where(first, 2, 1))
        kv_send(s, half, onward, 3, onward_device)
        kv_send(s, half, onward, jnp.where(first, 5, 4), sibling)
        kv_arrive(s, half, other, jnp.where(first, 1, 2))
        kv_send(s, half, other, jnp.where(first, 4, 5), sibling)

    def kv_far(s, half):
        kv_arrive(s, half, block(1, 1, 0), 3)
        kv_send(s, half, block(1, 1, 0), 6, sibling)

    def kv_all(s):
        for half in range(2):
            kv_arrive(s, half, block(0, 0, 1), 0)
            kv_arrive(s, half, block(1, 0, 1), 4)
            kv_arrive(s, half, block(0, 1, 1), 5)
            kv_arrive(s, half, block(1, 1, 1), 6)

    def normalize(s):
        total = jnp.zeros((size, 1), jnp.float32)
        for j in range(shards):
            wide = xg[j, rows_of(s)].astype(jnp.float32)
            total = total + jnp.sum(wide * wide, axis=1, keepdims=True)
        factor = lax.rsqrt(total / (shards * width) + norm_epsilon)
        for j in range(shards):
            normed[:, j * width : (j + 1) * width] = (xg[j, rows_of(s)].astype(jnp.float32) * factor).astype(
                jnp.bfloat16
            )

    def head_normed(acc, scale):
        parts = []
        for h in range(heads):
            head = acc[:, h * HD : (h + 1) * HD]
            factor = lax.rsqrt(jnp.mean(head * head, axis=1, keepdims=True) + head_epsilon) * scale
            parts.append((head * factor).astype(jnp.bfloat16))
        return parts

    def part_of(which):
        return jnp.dot(normed[...], w[which], preferred_element_type=jnp.float32)

    def project_kv(s):
        normalize(s)
        if s == 0:
            loads[1].wait()
        for h, value in enumerate(head_normed(part_of(1), 1.0)):
            kv[s, me, 0, :, h * HD : (h + 1) * HD] = value
        if s == 0:
            loads[2].wait()
        kv[s, me, 1] = part_of(2).astype(jnp.bfloat16)

    def project_q(s):
        if s == 0:
            loads[0].wait()
        for h, value in enumerate(head_normed(part_of(0), score_scale)):
            query[rows_of(s), h * HD : (h + 1) * HD] = value

    lane = lax.broadcasted_iota(jnp.int32, (1, period), 1)

    def begin_of(s):
        q_index = s * period + me * size + row
        begin = jnp.zeros((size, 1), jnp.int32)
        for d in range(docs):
            at = first_meta + d * (plane // docs)
            begin = jnp.where(q_index >= meta_ref[at, 0], meta_ref[at, 0], begin)
        return begin

    def attend(s, steps):
        begin = begin_of(s)

        def one_head(h, carry):
            at = pl.ds(pl.multiple_of(h * HD, HD), HD)
            lines = query[rows_of(s), at]
            top = jnp.zeros((size, HD), jnp.float32) if steps[0] == 0 else num[s, :, at]
            low = jnp.zeros((size, 1), jnp.float32) if steps[0] == 0 else den[s, :, at][:, :1]
            for t in steps:
                keys = kv[t, :, 0, :, at].reshape(period, HD)
                values = kv[t, :, 1, :, at].reshape(period, HD)
                scores = lax.dot_general(lines, keys, (((1,), (1,)), ((), ())), preferred_element_type=jnp.float32)
                allowed = lane >= begin - t * period
                if t == s:
                    allowed = allowed & (lane <= me * size + row)
                weights = jnp.where(allowed, jnp.exp(scores), 0.0)
                low = low + jnp.sum(weights, axis=1, keepdims=True)
                top = top + jnp.dot(weights.astype(jnp.bfloat16), values, preferred_element_type=jnp.float32)
            if steps[-1] == s:
                context[:, at] = (top / low).astype(jnp.bfloat16)
            else:
                num[s, :, at] = top
                den[s, :, at] = jnp.broadcast_to(low, (size, HD))
            return carry

        lax.fori_loop(0, heads, one_head, 0)

    def early(s, t):
        attend(s, [t])

    def late(s):
        attend(s, [s])

    def project_out(s):
        if s == 0:
            loads[3].wait()
        for j in range(shards):
            terms[s, j] = jnp.dot(
                context[...], wo[:, j * width : (j + 1) * width], preferred_element_type=jnp.float32
            ).astype(jnp.bfloat16)

    def sum_copy(s, part, way, d):
        land = from_right if way == 0 else from_left
        at = part_rows(part)
        return line_copy(
            terms.at[s, d, at],
            land.at[s, d, at],
            r_send.at[way, s, part, d],
            r_recv.at[way, s, part, d],
            left if way == 0 else right,
        )

    def sum_sent(way, d):
        return (z > d) if way == 0 else (z < d)

    def sum_first(s, part):
        for way in range(2):
            for k in range(last):

                @pl.when(z == (last if way == 0 else 0))
                def _():
                    sum_copy(s, part, way, k if way == 0 else last - k).start()

    def sum_round(s, part, r):
        at = part_rows(part)
        for way in range(2):
            land = from_right if way == 0 else from_left
            k = r - last + z if way == 0 else r - z
            d = k if way == 0 else last - k

            @pl.when((k >= 0) & ((z < last) if way == 0 else (z > 0)))
            def _():
                sum_copy(s, part, way, d).wait_recv()
                sums = terms[s, d, at].astype(jnp.float32) + land[s, d, at].astype(jnp.float32)
                terms[s, d, at] = sums.astype(jnp.bfloat16)
                sum_copy(s, part, way, d).start()

    def sum_final(s, part):
        at = part_rows(part)
        final[...] = terms[s, z, at].astype(jnp.float32)
        for way in range(2):
            land = from_right if way == 0 else from_left

            @pl.when((z < last) if way == 0 else (z > 0))
            def _():
                sum_copy(s, part, way, z).wait_recv()
                final[...] += land[s, z, at].astype(jnp.float32)

        o_ref[part_of_rows(s, part)] = final[...].astype(jnp.bfloat16)

    def sum_end():
        for s in range(stripes):
            for part in range(2):
                for way in range(2):
                    for d in range(shards):

                        @pl.when(sum_sent(way, d))
                        def _():
                            sum_copy(s, part, way, d).wait_send()

    steps = {
        "dsend": deal_send,
        "dwait": deal_wait,
        "dsel": deal_pick,
        "bsend": back_send,
        "bwait": back_wait,
        "first": feature_first,
        "hop": feature_hop,
        "pkv": project_kv,
        "pq": project_q,
        "own": kv_own,
        "near": kv_near,
        "far": kv_far,
        "all": kv_all,
        "early": early,
        "late": late,
        "out": project_out,
        "rfirst": sum_first,
        "round": sum_round,
        "final": sum_final,
    }
    for name, *at in ORDER:
        steps[name](*at)
    deal_end()
    feature_end()
    for copy in sent:
        copy.wait_send()
    sum_end()


def block(meta, first_meta, dealt, weight, out_weight, docs, shards, stripes, call):
    plane, size, width = dealt.shape
    rows = stripes * size
    head_width = weight.shape[2]
    full = out_weight.shape[1]
    sixteen = jnp.bfloat16
    dma = pltpu.SemaphoreType.DMA
    return pl.pallas_call(
        functools.partial(block_kernel, docs, first_meta),
        in_specs=[
            pl.BlockSpec(memory_space=pltpu.SMEM),
            pl.BlockSpec(memory_space=pltpu.VMEM),
            pl.BlockSpec(memory_space=pl.ANY),
            pl.BlockSpec(memory_space=pl.ANY),
        ],
        out_specs=pl.BlockSpec(memory_space=pltpu.VMEM),
        out_shape=jax.ShapeDtypeStruct((plane, size, width), sixteen),
        scratch_shapes=[
            pltpu.VMEM((plane, size, width), sixteen),
            pltpu.VMEM((rows, width), sixteen),
            pltpu.VMEM((rows, width), sixteen),
            pltpu.VMEM((plane, size, width), sixteen),
            pltpu.VMEM(weight.shape, sixteen),
            pltpu.VMEM(out_weight.shape, sixteen),
            pltpu.VMEM((shards, rows, width), sixteen),
            pltpu.VMEM((size, full), sixteen),
            pltpu.VMEM((rows, head_width), sixteen),
            pltpu.VMEM((stripes, plane, 2, size, head_width), sixteen),
            pltpu.VMEM((stripes, size, head_width), jnp.float32),
            pltpu.VMEM((stripes, size, head_width), jnp.float32),
            pltpu.VMEM((size, head_width), sixteen),
            pltpu.VMEM((stripes, shards, size, width), sixteen),
            pltpu.VMEM((stripes, shards, size, width), sixteen),
            pltpu.VMEM((stripes, shards, size, width), sixteen),
            pltpu.VMEM((size // 2, width), jnp.float32),
            dma((4,)),
            dma((2, stripes, 2, shards)),
            dma((2, stripes, 2, shards)),
            dma((stripes, 2, 7)),
            dma((stripes, 2, 7)),
            dma((2, stripes, 2, shards)),
            dma((2, stripes, 2, shards)),
            dma((2, plane)),
            dma((2, plane)),
            dma((2, plane)),
            dma((2, plane)),
        ],
        compiler_params=pltpu.CompilerParams(
            collective_id=call, has_side_effects=True, vmem_limit_bytes=VMEM_LIMIT
        ),
        cost_estimate=pl.CostEstimate(flops=10_000_000_000, bytes_accessed=100_000_000, transcendentals=0),
        name="block",
    )(meta, dealt, weight, out_weight)


LINES = 32


def count_kernel(depth_ref, place_ref, info_ref, mine, landed, send_sem, recv_sem):
    plane = landed.shape[0]
    lines, lanes = depth_ref.shape
    ctx_count = lax.axis_size("ctx")
    x, place = lax.axis_index("dp"), lax.axis_index("ctx")
    me = x * ctx_count + place

    def device(flip):
        return {"dp": x ^ (flip // ctx_count), "ctx": place ^ (flip % ctx_count)}

    barrier = pltpu.get_barrier_semaphore()
    for flip in range(1, plane):
        pl.semaphore_signal(barrier, inc=1, device_id=device(flip), device_id_type=pl.DeviceIdType.MESH)
    active = depth_ref[...] >= RECURSION
    ones = jnp.where(active, 1.0, 0.0)
    total = jnp.sum(jnp.sum(ones, axis=1, keepdims=True), axis=0, keepdims=True)
    mine[...] = jnp.broadcast_to(total, mine.shape).astype(jnp.int32)
    pl.semaphore_wait(barrier, plane - 1)

    def copy(flip, slot):
        return line_copy(mine, landed.at[slot], send_sem.at[flip], recv_sem.at[flip], device(flip))

    for flip in range(1, plane):
        copy(flip, me).start()
    landed[me] = mine[...]
    upto = lax.broadcasted_iota(jnp.int32, (lanes, lanes), 0) <= lax.broadcasted_iota(jnp.int32, (lanes, lanes), 1)
    inside = jnp.dot(
        ones.astype(jnp.bfloat16), jnp.where(upto, 1.0, 0.0).astype(jnp.bfloat16), preferred_element_type=jnp.float32
    )
    ahead = lax.broadcasted_iota(jnp.int32, (lines, lines), 1) < lax.broadcasted_iota(jnp.int32, (lines, lines), 0)
    line_total = jnp.broadcast_to(inside[:, lanes - 1 :], (lines, lanes))
    before = jnp.dot(
        jnp.where(ahead, 1.0, 0.0).astype(jnp.bfloat16),
        line_total.astype(jnp.bfloat16),
        preferred_element_type=jnp.float32,
    )
    for flip in range(1, plane):
        copy(flip, me ^ flip).wait_recv()
    start = jnp.zeros((1, lanes), jnp.int32)
    running = jnp.zeros((1, lanes), jnp.int32)
    for b in range(plane):
        info_ref[lines + b : lines + b + 1] = running
        count = landed[b, 0:1]
        start = start + jnp.where(me > b, count, 0)
        running = running + count
    for b in range(plane, info_ref.shape[0] - lines):
        info_ref[lines + b : lines + b + 1] = running
    base = (start & (CAP - 1)) + before.astype(jnp.int32)
    info_ref[:lines] = base
    place_ref[...] = jnp.where(active, base + inside.astype(jnp.int32) - 1, -1)
    for flip in range(1, plane):
        copy(flip, me).wait_send()


def count(depth, plane, call):
    lines = LINES
    lanes = depth.shape[0] // lines
    whole = jnp.int32
    return pl.pallas_call(
        count_kernel,
        in_specs=[pl.BlockSpec(memory_space=pltpu.VMEM)],
        out_specs=[pl.BlockSpec(memory_space=pltpu.VMEM)] * 2,
        out_shape=[
            jax.ShapeDtypeStruct((lines, lanes), whole),
            jax.ShapeDtypeStruct((lines + 16, lanes), whole),
        ],
        scratch_shapes=[
            pltpu.VMEM((8, lanes), whole),
            pltpu.VMEM((plane, 8, lanes), whole),
            pltpu.SemaphoreType.DMA((plane,)),
            pltpu.SemaphoreType.DMA((plane,)),
        ],
        compiler_params=pltpu.CompilerParams(collective_id=call, has_side_effects=True),
        name="count",
    )(depth.reshape(lines, lanes))


ALIGN = 16
GROUP = 2
LOADS = 8


def onehot_of(place_ref, at, floor, window):
    wanted = jnp.concatenate([place_ref[pl.ds(at + i, 1), :] for i in range(GROUP)], axis=1)
    spot = lax.broadcasted_iota(jnp.int32, (window, wanted.shape[1]), 0)
    return jnp.where(spot + floor == wanted, 1.0, 0.0).astype(jnp.bfloat16)


def compact_kernel(info_ref, place_ref, tokens_hbm, out_ref, tokens, buffer, sems):
    lines, lanes = place_ref.shape
    block_rows = GROUP * lanes
    window = block_rows + ALIGN
    chunk = tokens.shape[0] // LOADS
    loads = []
    for i in range(LOADS):
        rows = pl.ds(i * chunk, chunk)
        loads.append(pltpu.make_async_copy(tokens_hbm.at[rows], tokens.at[rows], sems.at[i]))
        loads[-1].start()
    start = info_ref[0, 0]
    edge = lax.broadcasted_iota(jnp.int32, (ALIGN, 1), 0)
    for i in range(lines // GROUP):
        if (i * block_rows) % chunk == 0:
            loads[i * block_rows // chunk].wait()
        base = info_ref[i * GROUP, 0]
        floor = pl.multiple_of(base - lax.rem(base, ALIGN), ALIGN)
        spread = onehot_of(place_ref, i * GROUP, floor, window)
        rows = tokens[i * block_rows : (i + 1) * block_rows]
        found = jnp.dot(spread, rows, preferred_element_type=jnp.float32)
        old = buffer[pl.ds(floor, ALIGN)].astype(jnp.float32)
        seam = jnp.where(edge < base - floor, old, found[:ALIGN])
        buffer[pl.ds(floor, ALIGN)] = seam.astype(jnp.bfloat16)
        buffer[pl.ds(floor + ALIGN, block_rows)] = found[ALIGN:].astype(jnp.bfloat16)
    plane, size, _ = out_ref.shape
    for b in range(plane):
        spot = b * size + lax.broadcasted_iota(jnp.int32, (size, 1), 0)
        low = buffer[b * size : (b + 1) * size].astype(jnp.float32)
        high = buffer[CAP + b * size : CAP + (b + 1) * size].astype(jnp.float32)
        out_ref[b] = jnp.where(spot >= start, low, high).astype(jnp.bfloat16)


def compact(info, places, tokens, plane):
    lines, lanes = places.shape
    width = tokens.shape[1]
    return pl.pallas_call(
        compact_kernel,
        in_specs=[
            pl.BlockSpec(memory_space=pltpu.SMEM),
            pl.BlockSpec(memory_space=pltpu.VMEM),
            pl.BlockSpec(memory_space=pl.ANY),
        ],
        out_specs=pl.BlockSpec(memory_space=pltpu.VMEM),
        out_shape=jax.ShapeDtypeStruct((plane, CAP // plane, width), tokens.dtype),
        scratch_shapes=[
            pltpu.VMEM(tokens.shape, tokens.dtype),
            pltpu.VMEM((2 * CAP + GROUP * lanes + ALIGN, width), tokens.dtype),
            pltpu.SemaphoreType.DMA((LOADS,)),
        ],
        compiler_params=pltpu.CompilerParams(vmem_limit_bytes=VMEM_LIMIT),
        name="compact",
    )(info, places, tokens)


def unpack_kernel(info_ref, place_ref, landed_ref, out_hbm, buffer, columns, out, sems):
    lines, lanes = place_ref.shape
    window = 2 * lanes
    buffer[:CAP] = landed_ref[...]
    buffer[CAP:] = landed_ref[: buffer.shape[0] - CAP]
    columns[...] = jnp.transpose(place_ref[...])
    spot = lax.broadcasted_iota(jnp.int32, (lanes, window), 1)
    chunk = out.shape[0] // LOADS
    stores = []
    for i in range(lines):
        base = info_ref[i, 0]
        floor = base - lax.rem(base, ALIGN)
        spread = jnp.where(columns[:, i : i + 1] - floor == spot, 1.0, 0.0).astype(jnp.bfloat16)
        rows = buffer[pl.ds(pl.multiple_of(lax.rem(floor, CAP), ALIGN), window)]
        out[i * lanes : (i + 1) * lanes] = jnp.dot(spread, rows, preferred_element_type=jnp.float32).astype(
            jnp.bfloat16
        )
        if (i + 1) * lanes % chunk == 0:
            at = pl.ds((i + 1) * lanes - chunk, chunk)
            stores.append(pltpu.make_async_copy(out.at[at], out_hbm.at[at], sems.at[len(stores)]))
            stores[-1].start()
    for store in stores:
        store.wait()


def unpack(info, places, landed, length):
    lines, lanes = places.shape
    width = landed.shape[1]
    return pl.pallas_call(
        unpack_kernel,
        in_specs=[
            pl.BlockSpec(memory_space=pltpu.SMEM),
            pl.BlockSpec(memory_space=pltpu.VMEM),
            pl.BlockSpec(memory_space=pltpu.VMEM),
        ],
        out_specs=pl.BlockSpec(memory_space=pl.ANY),
        out_shape=jax.ShapeDtypeStruct((length, width), landed.dtype),
        scratch_shapes=[
            pltpu.VMEM((CAP + 2 * lanes, width), landed.dtype),
            pltpu.VMEM((lanes, lines), jnp.int32),
            pltpu.VMEM((length, width), landed.dtype),
            pltpu.SemaphoreType.DMA((LOADS,)),
        ],
        compiler_params=pltpu.CompilerParams(vmem_limit_bytes=VMEM_LIMIT),
        name="unpack",
    )(info, places, landed)


def per_device(hidden, depth, qkv_weight, out_weight):
    tokens = hidden[0]
    local_len = tokens.shape[0]
    docs = lax.axis_size("dp")
    ctx_count = lax.axis_size("ctx")
    shards = lax.axis_size("tensor")
    plane = docs * ctx_count
    me = lax.axis_index("dp") * ctx_count + lax.axis_index("ctx")
    size = CAP // plane
    stripes = ACT_DEV // size

    if (docs, ctx_count) == (2, 4) and local_len % (LINES * 128) == 0 and stripes >= 2 and shards >= 2:
        places, info = count(depth[0], plane, 0)
        dealt = compact(info, places, tokens, plane)
        weight = jnp.transpose(qkv_weight, (1, 0, 2))
        landed = block(info, LINES, dealt, weight, out_weight, docs, shards, stripes, 1)
        return unpack(info, places, landed.reshape(CAP, -1), local_len)[None]

    active = depth[0] >= RECURSION
    ones = active.astype(jnp.int32)
    counts = lax.all_gather(jnp.sum(ones)[None], PLANE, axis=0, tiled=True)
    ends = jnp.cumsum(counts)
    starts = ends - counts
    rank = jnp.cumsum(ones) - 1
    slot = jnp.where(active, lax.rem(starts[me] + rank, CAP), -1)
    onehot = (jnp.arange(CAP, dtype=jnp.int32)[:, None] == slot[None, :]).astype(jnp.bfloat16)
    dealt = jnp.dot(onehot, tokens, preferred_element_type=jnp.float32).astype(jnp.bfloat16)
    received = lax.all_to_all(dealt.reshape(plane, size, -1), PLANE, 0, 0)

    index = (
        jnp.arange(stripes, dtype=jnp.int32)[:, None] * CAP
        + me * size
        + jnp.arange(size, dtype=jnp.int32)[None, :]
    )
    owned = (index[None] >= starts[:, None, None]) & (index[None] < ends[:, None, None])
    zero = jnp.zeros((), jnp.bfloat16)
    packed = jnp.where(owned[0][:, :, None], received[0][None], zero)
    for b in range(1, plane):
        packed = jnp.where(owned[b][:, :, None], received[b][None], packed)
    packed = packed.reshape(ACT_DEV, -1)

    chunks = 2
    chunk_stripes = stripes // chunks
    chunk_rows = ACT_DEV // chunks
    weight = jnp.transpose(qkv_weight, (1, 0, 2))
    meta = jnp.concatenate([starts[::ctx_count], me[None]]).astype(jnp.int32)
    rows_all = [
        lax.all_gather(packed[c * chunk_rows : (c + 1) * chunk_rows], "tensor", axis=0) for c in range(chunks)
    ]
    kvs, backs = [], []
    for c in range(chunks):
        queries, kv = project(rows_all[c], weight)
        kvs.append(lax.all_gather(kv, PLANE, axis=0))
        terms = attend(meta, queries, kvs, out_weight, shards, docs, chunk_stripes)
        backs.append(lax.psum_scatter(terms, "tensor", scatter_dimension=0))
    rows_back = jnp.concatenate(backs, axis=0)

    rows_back = rows_back.reshape(stripes, size, -1)
    returned = jnp.where(owned[:, 0][:, :, None], rows_back[0][None], zero)
    for k in range(1, stripes):
        returned = jnp.where(owned[:, k][:, :, None], rows_back[k][None], returned)
    landed = lax.all_to_all(returned, PLANE, 0, 0).reshape(CAP, -1)
    spread = (slot[:, None] == jnp.arange(CAP, dtype=jnp.int32)[None, :]).astype(jnp.bfloat16)
    update = jnp.dot(spread, landed, preferred_element_type=jnp.float32).astype(jnp.bfloat16)
    return update[None]


def solution(mesh):
    placed = (P("dp", "ctx", "tensor"), P("dp", "ctx"), P(None, None, "tensor"), P("tensor", None))
    return jax.shard_map(
        per_device, mesh=mesh, in_specs=placed, out_specs=P("dp", "ctx", "tensor"), check_vma=False
    )
```
